512 devices in a mesh: grp: 16 (over y, z_lo), col: 32 (over x, z_hi, core).
Axes of the slice: x: 4, y: 8, z: 8 (z_hi: 4, z_lo: 2; z = z_hi * 2 + z_lo), core: 2. Of those that a mesh axis runs over, the one named last changes fastest.
Arguments:
- border: bfloat16 [64, 384, 24576], P('grp', None, 'col'), may hold values from -0.30859375 to 0.30859375
- inverses: bfloat16 [64, 384, 384], P('grp'), may hold values from -0.3125 to 0.3125
- scen_map: int32 [16, 4], P('grp'), may hold values from 0 to 3, each once within a row
- owners: int32 [4], replicated, may hold values from 0 to 31
- slots: int32 [4], replicated, may hold values from 0 to 2
Outputs:
- schur_cols: float32 [4, 24576, 256], P(None, ('col', 'grp'))
The draws below stay inside these ranges and needn't reach their ends.
All inputs are finite; a program needn't handle non-finite values.
Results may differ from the reference program's by a relative error of at most 0.0029.
Values may be sent and summed in bfloat16 or wider, within the bound.
A program may use at most 64 MiB of HBM per device.

```python
import jax
import jax.numpy as jnp
from jax import lax

N = 24576
KO = 384
PW = 256
NP = 4
SG = 4
SCEN = 64
CW = 768
N_GRP = 16
N_COL = 32


def touch_ends(drawn, rng, low, largest):
    index_at = [jax.random.randint(jax.random.fold_in(rng, axis), (), 0, length) for axis, length in enumerate(drawn.shape)]
    longest = drawn.shape.index(max(drawn.shape))
    neighbour = index_at[:longest] + [(index_at[longest] + 1) % drawn.shape[longest]] + index_at[longest + 1:]
    return drawn.at[tuple(index_at)].set(low).at[tuple(neighbour)].set(largest)


def strengthened(array, stream_key, source, target, shards_of, factor):
    owner, partner = [(jnp.arange(array.shape[dim]) // (array.shape[dim] // shards_of)).reshape([-1 if axis == dim else 1 for axis in range(array.ndim)]) for dim in (source, target)]
    chosen = jax.random.permutation(stream_key, shards_of)[partner]
    strong = (owner == chosen) | (owner == (partner + shards_of // 2) % shards_of)
    return jnp.where(strong, factor * array, array)


def level_of(stream_key, dims, shards, low, top_value):
    gain, own = 1.0, jax.random.fold_in(stream_key, 6)
    for axis_at, blocks in shards:
        draws = jnp.exp(jax.random.uniform(jax.random.fold_in(own, axis_at), (blocks,), jnp.float32, low / len(shards), top_value / len(shards)))
        gain = gain * jnp.repeat(draws, dims[axis_at] // blocks).reshape([-1 if axis == axis_at else 1 for axis in range(len(dims))])
    return gain


def centred(rng, shape, width, reach, cuts=(), kind=jnp.bfloat16):
    values = width * jax.random.normal(rng, shape, jnp.float32)
    if cuts:
        values = values * level_of(rng, shape, cuts, -0.22, 0.18)
    return jnp.clip(values, -reach, reach).astype(kind)


def bell_draw_with(own_key, shape, spread, most, cuts, heavy, held_as=jnp.bfloat16):
    array = spread * jax.random.normal(own_key, shape, jnp.float32)
    if cuts:
        array = array * level_of(own_key, shape, cuts, -0.22, 0.18)
    return jnp.clip(strengthened(array, jax.random.fold_in(own_key, 3), *heavy), -most, most).astype(held_as)


def setup_inputs(seed: int = 0) -> dict:
    keys = jax.random.split(jax.random.key(seed), 6)
    return {
        "border": bell_draw_with(keys[0], (SCEN, KO, N), 0.051, 0.30859375, ((0, 16), (2, 32)), (0, 2, 32, 2.75)),
        "inverses": centred(keys[1], (SCEN, KO, KO), KO ** -0.5, 0.3125, ((0, 16),)),
        "scen_map": jax.vmap(lambda own: jax.random.permutation(own, SG))(jax.random.split(keys[2], N_GRP)).reshape((N_GRP, SG)).astype(jnp.int32),
        "owners": touch_ends(jax.random.randint(keys[3], (NP,), 0, N_COL), jax.random.fold_in(keys[3], 1), 0, N_COL - 1).astype(jnp.int32),
        "slots": touch_ends(jax.random.randint(keys[4], (NP,), 0, CW // PW), jax.random.fold_in(keys[4], 1), 0, (CW // PW) - 1).astype(jnp.int32),
    }


def reference(border, inverses, scen_map, owners, slots):
    groups = scen_map.shape[0]
    per_group = scen_map.shape[1]
    cols = []
    for p in range(NP):
        start = (owners[p] * CW + slots[p] * PW).astype(jnp.int32)
        panel = lax.dynamic_slice_in_dim(border, start, PW, 2)
        index = (jnp.arange(groups, dtype=jnp.int32)[:, None] * per_group + scen_map).reshape(-1).astype(jnp.int32)
        chosen = jnp.take(inverses, index, axis=0).astype(jnp.float32)
        applied = jnp.einsum("sij,sjc->sic", chosen, panel.astype(jnp.float32)).astype(jnp.bfloat16)
        total = jnp.zeros((border.shape[2], PW), jnp.float32)
        for g in range(groups):
            piece = border[g * per_group:(g + 1) * per_group].astype(jnp.float32)
            mine = applied[g * per_group:(g + 1) * per_group].astype(jnp.float32)
            total = total + jnp.einsum("sir,sic->rc", piece, mine)
        cols.append(total)
    return jnp.stack(cols)
```

```python
import functools

import jax
import jax.numpy as jnp
from jax import lax
from jax.experimental import pallas as pl
from jax.experimental.pallas import tpu as pltpu
from jax.sharding import PartitionSpec as P

X = 4
ZH = 4
Y = 8
LANE = 128


def greet(peers):
    barrier = pltpu.get_barrier_semaphore()
    for axis, peer in peers:
        pl.semaphore_signal(
            barrier, inc=1, device_id={axis: peer}, device_id_type=pl.DeviceIdType.MESH
        )
    pl.semaphore_wait(barrier, len(peers))


def remote(src, dst, send, recv, axis, peer):
    copy = pltpu.make_async_remote_copy(
        src_ref=src,
        dst_ref=dst,
        send_sem=send,
        recv_sem=recv,
        device_id={axis: peer},
        device_id_type=pl.DeviceIdType.MESH,
    )
    copy.start()
    return copy


def share_kernel(
    mine, chosen, border, out, turned,
    pair_in, x_out, x_in, z_sum, z_in, z_out, full, home,
    pair_s, pair_r, xs, xr, zs, zr, zgs, zgr, xgs, xgr, bs, br, outs,
):
    at = lax.axis_index("col")
    core = lax.rem(at, 2)
    zh = lax.rem(lax.div(at, 2), ZH)
    x = lax.div(at, 2 * ZH)
    way = 1 - 2 * core
    other = 1 - core

    def col(xx, zz, cc):
        return (xx * ZH + zz) * 2 + cc

    xa, xb, xf = lax.rem(x + way + X, X), lax.rem(x - way + X, X), lax.rem(x + 2, X)
    za, zb, zf = lax.rem(zh + way + ZH, ZH), lax.rem(zh - way + ZH, ZH), lax.rem(zh + 2, ZH)
    partner = col(x, zh, other)
    x_fwd, x_back = col(xa, zh, core), col(xb, zh, core)
    z_fwd, z_back = col(x, za, core), col(x, zb, core)
    greet([("col", d) for d in (partner, x_fwd, x_back, z_fwd, z_back)])

    sends = []
    pair = {}
    for k, s in enumerate((xf, xa, xb, x)):
        pair[k] = remote(mine.at[other, s], pair_in.at[s], pair_s.at[k], pair_r.at[k], "col", partner)
    pair[0].wait_recv()
    x_out[0] = mine[core, xf] + pair_in[xf]
    c0 = remote(x_out.at[0], x_in.at[0], xs.at[0], xr.at[0], "col", x_fwd)
    pair[1].wait_recv()
    x_out[1] = mine[core, xb] + pair_in[xb]
    c1 = remote(x_out.at[1], x_in.at[1], xs.at[1], xr.at[1], "col", x_back)
    pair[2].wait_recv()
    x_out[2] = mine[core, xa] + pair_in[xa]
    scen, depth, rows = border.shape
    turned[:, 0:depth] = border[0].T
    c0.wait_recv()
    x_out[3] = x_out[2] + x_in[0]
    c2 = remote(x_out.at[3], x_in.at[2], xs.at[2], xr.at[2], "col", x_fwd)
    for s in range(1, scen):
        turned[:, s * depth:(s + 1) * depth] = border[s].T
    pair[3].wait_recv()
    c1.wait_recv()
    z_sum[...] = mine[core, x] + pair_in[x] + x_in[1]
    c2.wait_recv()
    z_sum[...] = z_sum[...] + x_in[2]

    d0 = remote(z_sum.at[zf], z_in.at[0], zs.at[0], zr.at[0], "col", z_fwd)
    d1 = remote(z_sum.at[zb], z_in.at[1], zs.at[1], zr.at[1], "col", z_back)
    d0.wait_recv()
    z_out[...] = z_sum[za] + z_in[0]
    d2 = remote(z_out, z_in.at[2], zs.at[2], zr.at[2], "col", z_fwd)
    d1.wait_recv()
    part = z_sum[zh] + z_in[1]
    d2.wait_recv()
    part = part + z_in[2]
    home[...] = jnp.dot(chosen[x], part, preferred_element_type=jnp.float32).astype(jnp.bfloat16)

    keep = pltpu.make_async_copy(home, full.at[core, x, zh], outs.at[0, 0])
    keep.start()
    e0 = remote(home, full.at[core, x, zh], zgs.at[0], zgr.at[0], "col", z_fwd)
    e1 = remote(home, full.at[core, x, zh], zgs.at[1], zgr.at[1], "col", z_back)
    e0.wait_recv()
    e2 = remote(full.at[core, x, zb], full.at[core, x, zb], zgs.at[2], zgr.at[2], "col", z_fwd)
    e1.wait_recv()
    keep.wait()
    e2.wait_recv()

    stores = []

    def store(cc, s, slot):
        for q in range(4):
            copy = pltpu.make_async_copy(
                full.at[cc, s, q],
                out.at[cc, q // 2, s, :, pl.ds((q % 2) * LANE, LANE)],
                outs.at[slot, q],
            )
            copy.start()
            stores.append(copy)

    def both(s, k):
        sends.append(
            remote(full.at[core, s], full.at[core, s], bs.at[k], br.at[k], "col", partner)
        )
        store(core, s, k)

    g0 = remote(full.at[core, x], full.at[core, x], xgs.at[0], xgr.at[0], "col", x_fwd)
    g1 = remote(full.at[core, x], full.at[core, x], xgs.at[1], xgr.at[1], "col", x_back)
    both(x, 0)
    g0.wait_recv()
    g2 = remote(full.at[core, xb], full.at[core, xb], xgs.at[2], xgr.at[2], "col", x_fwd)
    both(xb, 1)
    g1.wait_recv()
    both(xa, 2)
    sends[0].wait_recv()
    store(other, x, 4)
    sends[1].wait_recv()
    store(other, xa, 5)
    sends[2].wait_recv()
    store(other, xb, 6)
    g2.wait_recv()
    both(xf, 3)
    sends[3].wait_recv()
    store(other, xf, 7)
    for copy in [pair[k] for k in range(4)] + [c0, c1, c2, d0, d1, d2, e0, e1, e2, g0, g1, g2] + sends:
        copy.wait_send()
    for copy in stores:
        copy.wait()


def share(mine, chosen, border):
    _, xn, zn, depth, lane = mine.shape
    scen, _, rows = border.shape
    piece = (depth, lane)
    chunk = (zn,) + piece
    bf = jnp.bfloat16
    dma = pltpu.SemaphoreType.DMA
    vm = pl.BlockSpec(memory_space=pltpu.VMEM)
    return pl.pallas_call(
        share_kernel,
        out_shape=(
            jax.ShapeDtypeStruct((2, 2, scen, depth, 2 * lane), bf),
            jax.ShapeDtypeStruct((rows, scen * depth), bf),
        ),
        in_specs=[vm, vm, vm],
        out_specs=(pl.BlockSpec(memory_space=pl.ANY), vm),
        scratch_shapes=[
            pltpu.VMEM((xn,) + chunk, bf),
            pltpu.VMEM((4,) + chunk, bf),
            pltpu.VMEM((3,) + chunk, bf),
            pltpu.VMEM(chunk, bf),
            pltpu.VMEM((3,) + piece, bf),
            pltpu.VMEM(piece, bf),
            pltpu.VMEM((2, xn) + chunk, bf),
            pltpu.VMEM(piece, bf),
            dma((4,)), dma((4,)),
            dma((3,)), dma((3,)),
            dma((3,)), dma((3,)),
            dma((3,)), dma((3,)),
            dma((3,)), dma((3,)),
            dma((4,)), dma((4,)),
            dma((8, 4)),
        ],
        compiler_params=pltpu.CompilerParams(
            collective_id=0, has_side_effects=True, vmem_limit_bytes=48 * 1024 * 1024
        ),
    )(mine, chosen, border)


def reduce_kernel(
    turned, shared, out,
    own, a_out, a_in, b_out, b_in, half_out, half_in,
    a_s, a_r, b_s, b_r, h_s, h_r,
):
    at = lax.axis_index("grp")
    zl = lax.rem(at, 2)
    y = lax.div(at, 2)
    core = lax.rem(lax.axis_index("col"), 2)
    way = 1 - 2 * core

    def ring(step):
        return lax.rem(y + step * way + 2 * Y, Y)

    fwd, back = ring(1) * 2 + zl, ring(-1) * 2 + zl
    mate = y * 2 + (1 - zl)
    greet([("grp", d) for d in (fwd, back, mate)])

    panels = shared.shape[0]
    far, near = Y // 2, Y // 2 - 1
    sent = []
    ahead, behind, halves = {}, {}, {}

    def product(p):
        whole = jnp.dot(turned[...], shared[p], preferred_element_type=jnp.float32)
        own[p] = whole.reshape(own.shape[1:])

    def hop(p, t):
        term = own[p, ring(far - t)]
        if t > 0:
            ahead[p].wait_recv()
            term = term + a_in[p, t - 1].astype(jnp.float32)
        a_out[p, t] = term.astype(jnp.bfloat16)
        ahead[p] = remote(a_out.at[p, t], a_in.at[p, t], a_s.at[p, t], a_r.at[p, t], "grp", fwd)
        sent.append(ahead[p])
        if t < near:
            term = own[p, ring(t - near)]
            if t > 0:
                behind[p].wait_recv()
                term = term + b_in[p, t - 1].astype(jnp.float32)
            b_out[p, t] = term.astype(jnp.bfloat16)
            behind[p] = remote(b_out.at[p, t], b_in.at[p, t], b_s.at[p, t], b_r.at[p, t], "grp", back)
            sent.append(behind[p])

    def meet(p):
        behind[p].wait_recv()
        ahead[p].wait_recv()

        def total(z):
            return (
                own[p, y, z]
                + a_in[p, far - 1, z].astype(jnp.float32)
                + b_in[p, near - 1, z].astype(jnp.float32)
            )

        half_out[p] = total(1 - zl)
        halves[p] = remote(half_out.at[p], half_in.at[p], h_s.at[p], h_r.at[p], "grp", mate)
        sent.append(halves[p])
        out[p] = total(zl)

    def finish(p):
        halves[p].wait_recv()
        out[p] = out[p] + half_in[p]

    for u in range(panels + far + 1):
        if u < panels:
            product(u)
        for p in range(panels):
            t = u - p
            if 0 <= t < far:
                hop(p, t)
            elif t == far:
                meet(p)
            elif t == far + 1:
                finish(p)
    for copy in sent:
        copy.wait_send()


def reduce_over_groups(turned, shared):
    panels, _, width = shared.shape
    rows = turned.shape[0] // (2 * Y)
    block = (2, rows, width)
    far, near = Y // 2, Y // 2 - 1
    f32, bf = jnp.float32, jnp.bfloat16
    dma = pltpu.SemaphoreType.DMA
    vm = pl.BlockSpec(memory_space=pltpu.VMEM)
    return pl.pallas_call(
        reduce_kernel,
        out_shape=jax.ShapeDtypeStruct((panels, rows, width), f32),
        in_specs=[vm, vm],
        out_specs=vm,
        scratch_shapes=[
            pltpu.VMEM((panels, Y) + block, f32),
            pltpu.VMEM((panels, far) + block, bf),
            pltpu.VMEM((panels, far) + block, bf),
            pltpu.VMEM((panels, near) + block, bf),
            pltpu.VMEM((panels, near) + block, bf),
            pltpu.VMEM((panels, rows, width), f32),
            pltpu.VMEM((panels, rows, width), f32),
            dma((panels, far)), dma((panels, far)),
            dma((panels, near)), dma((panels, near)),
            dma((panels,)), dma((panels,)),
        ],
        compiler_params=pltpu.CompilerParams(
            collective_id=1, has_side_effects=True, vmem_limit_bytes=48 * 1024 * 1024
        ),
    )(turned, shared)


def on_device(border, inverses, scen_map, owners, slots):
    scen, depth, _ = border.shape
    width = 2 * LANE
    chosen = jnp.take(inverses, scen_map[0], axis=0)
    me = lax.axis_index("col")
    panels = []
    for p in range(owners.shape[0]):
        panel = lax.dynamic_slice_in_dim(border, slots[p] * width, width, 2)
        panels.append(jnp.where(owners[p] == me, panel, jnp.zeros_like(panel)))
    mine = jnp.stack(panels).reshape(2, 2, scen, depth, 2, LANE)
    mine = mine.transpose(0, 2, 1, 4, 3, 5).reshape(2, scen, 4, depth, LANE)
    shared, turned = share(mine, chosen, border)
    shared = shared.reshape(4, scen * depth, width)
    return reduce_over_groups(turned, shared)


def solution(mesh):
    return jax.shard_map(
        on_device,
        mesh=mesh,
        in_specs=(P("grp", None, "col"), P("grp", None, None), P("grp", None), P(), P()),
        out_specs=P(None, ("col", "grp"), None),
        check_vma=False,
    )
```

```python
import functools

import jax
import jax.numpy as jnp
from jax import lax
from jax.experimental import pallas as pl
from jax.experimental.pallas import tpu as pltpu
from jax.sharding import PartitionSpec as P

X = 4
ZH = 4
Y = 8
LANE = 128
TILE = 16


def greet(peers):
    barrier = pltpu.get_barrier_semaphore()
    for axis, peer in peers:
        pl.semaphore_signal(
            barrier, inc=1, device_id={axis: peer}, device_id_type=pl.DeviceIdType.MESH
        )
    pl.semaphore_wait(barrier, len(peers))


def remote(src, dst, send, recv, axis, peer):
    copy = pltpu.make_async_remote_copy(
        src_ref=src,
        dst_ref=dst,
        send_sem=send,
        recv_sem=recv,
        device_id={axis: peer},
        device_id_type=pl.DeviceIdType.MESH,
    )
    copy.start()
    return copy


def share_kernel(
    owners, slots, scen_map, border, inverses, out, turned,
    marks, picked, pair_out, pair_in, x_out, x_in, z_sum, z_in, z_out, full, home,
    pair_s, pair_r, xs, xr, zs, zr, zgs, zgr, xgs, xgr, bs, br, outs,
):
    at = lax.axis_index("col")
    core = lax.rem(at, 2)
    zh = lax.rem(lax.div(at, 2), ZH)
    x = lax.div(at, 2 * ZH)
    way = 1 - 2 * core
    other = 1 - core

    def col(xx, zz, cc):
        return (xx * ZH + zz) * 2 + cc

    def flag(left, right):
        same = jnp.full((TILE, LANE), left, jnp.int32) == jnp.full((TILE, LANE), right, jnp.int32)
        return jnp.where(same, 1.0, 0.0)

    tiles = border.shape[1] // TILE
    for p in range(owners.shape[0]):
        for k in range(3):
            marks[p, k] = (flag(owners[p], at) * flag(slots[p], k)).astype(jnp.bfloat16)

    def panel(cc, s, q):
        total = None
        for k in range(3):
            start = k * 2 * LANE + (q % 2) * LANE
            block = border[s, :, start:start + LANE].reshape(tiles, TILE, LANE)
            term = block * marks[2 * cc + q // 2, k][None]
            total = term if total is None else total + term
        return total.reshape(tiles * TILE, LANE)

    xa, xb, xf = lax.rem(x + way + X, X), lax.rem(x - way + X, X), lax.rem(x + 2, X)
    za, zb, zf = lax.rem(zh + way + ZH, ZH), lax.rem(zh - way + ZH, ZH), lax.rem(zh + 2, ZH)
    partner = col(x, zh, other)
    x_fwd, x_back = col(xa, zh, core), col(xb, zh, core)
    z_fwd, z_back = col(x, za, core), col(x, zb, core)
    greet([("col", d) for d in (partner, x_fwd, x_back, z_fwd, z_back)])

    sends = []
    pair = {}
    for k, s in enumerate((xf, xa, xb, x)):
        for q in range(4):
            pair_out[k, q] = panel(other, s, q)
        pair[k] = remote(pair_out.at[k], pair_in.at[s], pair_s.at[k], pair_r.at[k], "col", partner)
    pair[0].wait_recv()
    for q in range(4):
        x_out[0, q] = panel(core, xf, q) + pair_in[xf, q]
    c0 = remote(x_out.at[0], x_in.at[0], xs.at[0], xr.at[0], "col", x_fwd)
    pair[1].wait_recv()
    for q in range(4):
        x_out[1, q] = panel(core, xb, q) + pair_in[xb, q]
    c1 = remote(x_out.at[1], x_in.at[1], xs.at[1], xr.at[1], "col", x_back)
    pair[2].wait_recv()
    for q in range(4):
        x_out[2, q] = panel(core, xa, q) + pair_in[xa, q]
    scen, depth, rows = border.shape
    turned[:, 0:depth] = border[0].T
    for lane in range(0, depth, LANE):
        total = None
        for k in range(scen):
            mark = flag(scen_map[0, x], k).astype(jnp.bfloat16)
            term = inverses[k, :, lane:lane + LANE].reshape(tiles, TILE, LANE) * mark[None]
            total = term if total is None else total + term
        picked[:, lane:lane + LANE] = total.reshape(depth, LANE)
    c0.wait_recv()
    x_out[3] = x_out[2] + x_in[0]
    c2 = remote(x_out.at[3], x_in.at[2], xs.at[2], xr.at[2], "col", x_fwd)
    for s in range(1, scen):
        turned[:, s * depth:(s + 1) * depth] = border[s].T
    pair[3].wait_recv()
    c1.wait_recv()
    for q in range(4):
        z_sum[q] = panel(core, x, q) + pair_in[x, q] + x_in[1, q]
    c2.wait_recv()
    z_sum[...] = z_sum[...] + x_in[2]

    d0 = remote(z_sum.at[zf], z_in.at[0], zs.at[0], zr.at[0], "col", z_fwd)
    d1 = remote(z_sum.at[zb], z_in.at[1], zs.at[1], zr.at[1], "col", z_back)
    d0.wait_recv()
    z_out[...] = z_sum[za] + z_in[0]
    d2 = remote(z_out, z_in.at[2], zs.at[2], zr.at[2], "col", z_fwd)
    d1.wait_recv()
    part = z_sum[zh] + z_in[1]
    d2.wait_recv()
    part = part + z_in[2]
    home[...] = jnp.dot(picked[...], part, preferred_element_type=jnp.float32).astype(jnp.bfloat16)

    keep = pltpu.make_async_copy(home, full.at[core, x, zh], outs.at[0, 0])
    keep.start()
    e0 = remote(home, full.at[core, x, zh], zgs.at[0], zgr.at[0], "col", z_fwd)
    e1 = remote(home, full.at[core, x, zh], zgs.at[1], zgr.at[1], "col", z_back)
    e0.wait_recv()
    e2 = remote(full.at[core, x, zb], full.at[core, x, zb], zgs.at[2], zgr.at[2], "col", z_fwd)
    e1.wait_recv()
    keep.wait()
    e2.wait_recv()

    stores = []

    def store(cc, s, slot):
        for q in range(4):
            copy = pltpu.make_async_copy(
                full.at[cc, s, q],
                out.at[cc, q // 2, s, :, pl.ds((q % 2) * LANE, LANE)],
                outs.at[slot, q],
            )
            copy.start()
            stores.append(copy)

    def both(s, k):
        sends.append(
            remote(full.at[core, s], full.at[core, s], bs.at[k], br.at[k], "col", partner)
        )
        store(core, s, k)

    g0 = remote(full.at[core, x], full.at[core, x], xgs.at[0], xgr.at[0], "col", x_fwd)
    g1 = remote(full.at[core, x], full.at[core, x], xgs.at[1], xgr.at[1], "col", x_back)
    both(x, 0)
    g0.wait_recv()
    g2 = remote(full.at[core, xb], full.at[core, xb], xgs.at[2], xgr.at[2], "col", x_fwd)
    both(xb, 1)
    g1.wait_recv()
    both(xa, 2)
    sends[0].wait_recv()
    store(other, x, 4)
    sends[1].wait_recv()
    store(other, xa, 5)
    sends[2].wait_recv()
    store(other, xb, 6)
    g2.wait_recv()
    both(xf, 3)
    sends[3].wait_recv()
    store(other, xf, 7)
    for copy in [pair[k] for k in range(4)] + [c0, c1, c2, d0, d1, d2, e0, e1, e2, g0, g1, g2] + sends:
        copy.wait_send()
    for copy in stores:
        copy.wait()


def share(owners, slots, scen_map, border, inverses):
    scen, depth, rows = border.shape
    lane, xn = LANE, X
    piece = (depth, lane)
    chunk = (ZH,) + piece
    bf = jnp.bfloat16
    dma = pltpu.SemaphoreType.DMA
    vm = pl.BlockSpec(memory_space=pltpu.VMEM)
    sm = pl.BlockSpec(memory_space=pltpu.SMEM)
    return pl.pallas_call(
        share_kernel,
        out_shape=(
            jax.ShapeDtypeStruct((2, 2, scen, depth, 2 * lane), bf),
            jax.ShapeDtypeStruct((rows, scen * depth), bf),
        ),
        in_specs=[sm, sm, sm, vm, vm],
        out_specs=(vm, vm),
        scratch_shapes=[
            pltpu.VMEM((4, 3, TILE, LANE), bf),
            pltpu.VMEM((depth, depth), bf),
            pltpu.VMEM((xn,) + chunk, bf),
            pltpu.VMEM((xn,) + chunk, bf),
            pltpu.VMEM((4,) + chunk, bf),
            pltpu.VMEM((3,) + chunk, bf),
            pltpu.VMEM(chunk, bf),
            pltpu.VMEM((3,) + piece, bf),
            pltpu.VMEM(piece, bf),
            pltpu.VMEM((2, xn) + chunk, bf),
            pltpu.VMEM(piece, bf),
            dma((4,)), dma((4,)),
            dma((3,)), dma((3,)),
            dma((3,)), dma((3,)),
            dma((3,)), dma((3,)),
            dma((3,)), dma((3,)),
            dma((4,)), dma((4,)),
            dma((8, 4)),
        ],
        compiler_params=pltpu.CompilerParams(
            collective_id=0, has_side_effects=True, vmem_limit_bytes=24 * 1024 * 1024
        ),
    )(owners, slots, scen_map, border, inverses)


def reduce_kernel(
    turned, shared, out,
    own, a_out, a_in, b_out, b_in, half_out, half_in,
    a_s, a_r, b_s, b_r, h_s, h_r,
):
    at = lax.axis_index("grp")
    zl = lax.rem(at, 2)
    y = lax.div(at, 2)
    core = lax.rem(lax.axis_index("col"), 2)
    way = 1 - 2 * core

    def ring(step):
        return lax.rem(y + step * way + 2 * Y, Y)

    fwd, back = ring(1) * 2 + zl, ring(-1) * 2 + zl
    mate = y * 2 + (1 - zl)
    panels = shared.shape[0]
    greet([("grp", d) for d in (fwd, back, mate)])

    far, near = Y // 2, Y // 2 - 1
    sent = []
    ahead, behind, halves = {}, {}, {}

    def product(p):
        whole = jnp.dot(turned[...], shared[p], preferred_element_type=jnp.float32)
        own[p] = whole.reshape(own.shape[1:])

    def hop(p, t):
        term = own[p, ring(far - t)]
        if t > 0:
            ahead[p].wait_recv()
            term = term + a_in[p, t - 1].astype(jnp.float32)
        a_out[p, t] = term.astype(jnp.bfloat16)
        ahead[p] = remote(a_out.at[p, t], a_in.at[p, t], a_s.at[p, t], a_r.at[p, t], "grp", fwd)
        sent.append(ahead[p])
        if t < near:
            term = own[p, ring(t - near)]
            if t > 0:
                behind[p].wait_recv()
                term = term + b_in[p, t - 1].astype(jnp.float32)
            b_out[p, t] = term.astype(jnp.bfloat16)
            behind[p] = remote(b_out.at[p, t], b_in.at[p, t], b_s.at[p, t], b_r.at[p, t], "grp", back)
            sent.append(behind[p])

    def meet(p):
        behind[p].wait_recv()
        ahead[p].wait_recv()

        def total(z):
            return (
                own[p, y, z]
                + a_in[p, far - 1, z].astype(jnp.float32)
                + b_in[p, near - 1, z].astype(jnp.float32)
            )

        half_out[p] = total(1 - zl)
        halves[p] = remote(half_out.at[p], half_in.at[p], h_s.at[p], h_r.at[p], "grp", mate)
        sent.append(halves[p])
        out[p] = total(zl)

    def finish(p):
        halves[p].wait_recv()
        out[p] = out[p] + half_in[p]

    for u in range(panels + far + 1):
        if u < panels:
            product(u)
        for p in range(panels):
            t = u - p
            if 0 <= t < far:
                hop(p, t)
            elif t == far:
                meet(p)
            elif t == far + 1:
                finish(p)
    for copy in sent:
        copy.wait_send()


def reduce_over_groups(turned, shared):
    panels, _, width = shared.shape
    rows = turned.shape[0] // (2 * Y)
    block = (2, rows, width)
    far, near = Y // 2, Y // 2 - 1
    f32, bf = jnp.float32, jnp.bfloat16
    dma = pltpu.SemaphoreType.DMA
    vm = pl.BlockSpec(memory_space=pltpu.VMEM)
    return pl.pallas_call(
        reduce_kernel,
        out_shape=jax.ShapeDtypeStruct((panels, rows, width), f32),
        in_specs=[vm, vm],
        out_specs=vm,
        scratch_shapes=[
            pltpu.VMEM((panels, Y) + block, f32),
            pltpu.VMEM((panels, far) + block, bf),
            pltpu.VMEM((panels, far) + block, bf),
            pltpu.VMEM((panels, near) + block, bf),
            pltpu.VMEM((panels, near) + block, bf),
            pltpu.VMEM((panels, rows, width), f32),
            pltpu.VMEM((panels, rows, width), f32),
            dma((panels, far)), dma((panels, far)),
            dma((panels, near)), dma((panels, near)),
            dma((panels,)), dma((panels,)),
        ],
        compiler_params=pltpu.CompilerParams(
            collective_id=1, has_side_effects=True, vmem_limit_bytes=24 * 1024 * 1024
        ),
    )(turned, shared)


def on_device(border, inverses, scen_map, owners, slots):
    scen, depth, _ = border.shape
    shared, turned = share(owners, slots, scen_map, border, inverses)
    shared = shared.reshape(4, scen * depth, 2 * LANE)
    return reduce_over_groups(turned, shared)


def solution(mesh):
    return jax.shard_map(
        on_device,
        mesh=mesh,
        in_specs=(P("grp", None, "col"), P("grp", None, None), P("grp", None), P(), P()),
        out_specs=P(None, ("col", "grp"), None),
        check_vma=False,
    )
```

```python
import functools

import jax
import jax.numpy as jnp
from jax import lax
from jax.experimental import pallas as pl
from jax.experimental.pallas import tpu as pltpu
from jax.sharding import PartitionSpec as P

X = 4
ZH = 4
Y = 8
LANE = 128
TILE = 16


def greet(peers):
    barrier = pltpu.get_barrier_semaphore()
    for axis, peer in peers:
        pl.semaphore_signal(
            barrier, inc=1, device_id={axis: peer}, device_id_type=pl.DeviceIdType.MESH
        )
    pl.semaphore_wait(barrier, len(peers))


def remote(src, dst, send, recv, axis, peer):
    copy = pltpu.make_async_remote_copy(
        src_ref=src,
        dst_ref=dst,
        send_sem=send,
        recv_sem=recv,
        device_id={axis: peer},
        device_id_type=pl.DeviceIdType.MESH,
    )
    copy.start()
    return copy


def share_kernel(
    owners, slots, scen_map, border, inverses, full, turned,
    marks, picked, pair_out, pair_in, x_out, x_own, x_in, z_sum, z_in, z_out, home,
    pair_s, pair_r, xs, xr, zs, zr, zgs, zgr, xgs, xgr, bs, br,
):
    at = lax.axis_index("col")
    core = lax.rem(at, 2)
    zh = lax.rem(lax.div(at, 2), ZH)
    x = lax.div(at, 2 * ZH)
    way = 1 - 2 * core
    other = 1 - core

    def col(xx, zz, cc):
        return (xx * ZH + zz) * 2 + cc

    def flag(left, right):
        same = jnp.full((TILE, LANE), left, jnp.int32) == jnp.full((TILE, LANE), right, jnp.int32)
        return jnp.where(same, 1.0, 0.0)

    scen, depth, _ = border.shape
    parts = depth // LANE
    tiles = LANE // TILE
    for p in range(owners.shape[0]):
        for k in range(3):
            marks[p, k] = (flag(owners[p], at) * flag(slots[p], k)).astype(jnp.bfloat16)

    def panel(cc, s, r, q):
        total = None
        for k in range(3):
            start = k * 2 * LANE + (q % 2) * LANE
            block = border[s, r * LANE:(r + 1) * LANE, start:start + LANE]
            block = block.reshape(tiles, TILE, LANE)
            term = block * marks[2 * cc + q // 2, k][None]
            total = term if total is None else total + term
        return total.reshape(LANE, LANE)

    def turn(s):
        turned[:, s * depth:(s + 1) * depth] = border[s].T

    xa, xb, xf = lax.rem(x + way + X, X), lax.rem(x - way + X, X), lax.rem(x + 2, X)
    za, zb, zf = lax.rem(zh + way + ZH, ZH), lax.rem(zh - way + ZH, ZH), lax.rem(zh + 2, ZH)
    partner = col(x, zh, other)
    x_fwd, x_back = col(xa, zh, core), col(xb, zh, core)
    z_fwd, z_back = col(x, za, core), col(x, zb, core)
    greet([("col", d) for d in (partner, x_fwd, x_back, z_fwd, z_back)])

    order = range(parts)
    sends = []

    def send(*args):
        copy = remote(*args)
        sends.append(copy)
        return copy

    pair = {}
    for k, s in enumerate((xf, xa, xb, x)):
        for r in order:
            for q in range(ZH):
                pair_out[k, r, q] = panel(other, s, r, q)
            pair[k, r] = send(
                pair_out.at[k, r], pair_in.at[s, r], pair_s.at[k, r], pair_r.at[k, r], "col", partner
            )

    def joined(k, s, r, q):
        return panel(core, s, r, q) + pair_in[s, r, q]

    c = {}
    for k, s, peer in ((0, xf, x_fwd), (1, xb, x_back)):
        for r in order:
            pair[k, r].wait_recv()
            for q in range(ZH):
                x_out[k, r, q] = joined(k, s, r, q)
            c[k, r] = send(x_out.at[k, r], x_in.at[k, r], xs.at[k, r], xr.at[k, r], "col", peer)
    for r in order:
        pair[2, r].wait_recv()
        for q in range(ZH):
            x_own[0, r, q] = joined(2, xa, r, q)
    turn(0)
    for r in order:
        c[0, r].wait_recv()
        for q in range(ZH):
            x_out[2, r, q] = x_own[0, r, q] + x_in[0, r, q]
        c[2, r] = send(x_out.at[2, r], x_in.at[2, r], xs.at[2, r], xr.at[2, r], "col", x_fwd)
    for lane in range(0, depth, LANE):
        for r in order:
            total = None
            for k in range(scen):
                mark = flag(scen_map[0, x], k).astype(jnp.bfloat16)
                block = inverses[k, r * LANE:(r + 1) * LANE, lane:lane + LANE]
                term = block.reshape(tiles, TILE, LANE) * mark[None]
                total = term if total is None else total + term
            picked[r * LANE:(r + 1) * LANE, lane:lane + LANE] = total.reshape(LANE, LANE)
    for r in order:
        pair[3, r].wait_recv()
        c[1, r].wait_recv()
        for q in range(ZH):
            x_own[1, r, q] = joined(3, x, r, q) + x_in[1, r, q]
    turn(1)

    d = {}

    def relay(r):
        d[0, r].wait_recv()
        z_out[r] = z_sum[r, za] + z_in[0, r]
        d[2, r] = send(z_out.at[r], z_in.at[2, r], zs.at[2, r], zr.at[2, r], "col", z_fwd)

    for r in order:
        c[2, r].wait_recv()
        for q in range(ZH):
            z_sum[r, q] = x_own[1, r, q] + x_in[2, r, q]
        d[0, r] = send(z_sum.at[r, zf], z_in.at[0, r], zs.at[0, r], zr.at[0, r], "col", z_fwd)
        d[1, r] = send(z_sum.at[r, zb], z_in.at[1, r], zs.at[1, r], zr.at[1, r], "col", z_back)
        if r > 0:
            relay(r - 1)
    relay(parts - 1)
    result = None
    for r in order:
        d[1, r].wait_recv()
        part = z_sum[r, zh] + z_in[1, r]
        d[2, r].wait_recv()
        part = part + z_in[2, r]
        term = jnp.dot(
            picked[:, r * LANE:(r + 1) * LANE], part, preferred_element_type=jnp.float32
        )
        result = term if result is None else result + term

    e = {}
    for r in order:
        home[r] = result[r * LANE:(r + 1) * LANE].astype(jnp.bfloat16)
        for k, peer in ((0, z_fwd), (1, z_back)):
            e[k, r] = send(
                home.at[r], full.at[core, x, r, zh], zgs.at[k, r], zgr.at[k, r], "col", peer
            )
        full[core, x, r, zh] = home[r]

    def pass_on(k, s, r, sent, got, axis, peer):
        return send(full.at[core, s, r], full.at[core, s, r], sent.at[k, r], got.at[k, r], axis, peer)

    for r in order:
        e[0, r].wait_recv()
        held = full.at[core, x, r, zb]
        e[2, r] = send(held, held, zgs.at[2, r], zgr.at[2, r], "col", z_fwd)
    g, h = {}, {}
    for r in order:
        e[1, r].wait_recv()
        e[2, r].wait_recv()
        g[0, r] = pass_on(0, x, r, xgs, xgr, "col", x_fwd)
        g[1, r] = pass_on(1, x, r, xgs, xgr, "col", x_back)
        h[0, r] = pass_on(0, x, r, bs, br, "col", partner)
    turn(2)
    for r in order:
        g[0, r].wait_recv()
        g[2, r] = pass_on(2, xb, r, xgs, xgr, "col", x_fwd)
        h[1, r] = pass_on(1, xb, r, bs, br, "col", partner)
    turn(3)
    for r in order:
        g[1, r].wait_recv()
        h[2, r] = pass_on(2, xa, r, bs, br, "col", partner)
    for r in order:
        g[2, r].wait_recv()
        h[3, r] = pass_on(3, xf, r, bs, br, "col", partner)
    for copy in h.values():
        copy.wait_recv()
    for copy in sends:
        copy.wait_send()


def share(owners, slots, scen_map, border, inverses):
    scen, depth, rows = border.shape
    parts = depth // LANE
    piece = (parts, LANE, LANE)
    chunk = (parts, ZH, LANE, LANE)
    bf = jnp.bfloat16
    dma = pltpu.SemaphoreType.DMA
    vm = pl.BlockSpec(memory_space=pltpu.VMEM)
    sm = pl.BlockSpec(memory_space=pltpu.SMEM)
    return pl.pallas_call(
        share_kernel,
        out_shape=(
            jax.ShapeDtypeStruct((2, X) + chunk, bf),
            jax.ShapeDtypeStruct((rows, scen * depth), bf),
        ),
        in_specs=[sm, sm, sm, vm, vm],
        out_specs=(vm, vm),
        scratch_shapes=[
            pltpu.VMEM((4, 3, TILE, LANE), bf),
            pltpu.VMEM((depth, depth), bf),
            pltpu.VMEM((X,) + chunk, bf),
            pltpu.VMEM((X,) + chunk, bf),
            pltpu.VMEM((3,) + chunk, bf),
            pltpu.VMEM((2,) + chunk, bf),
            pltpu.VMEM((3,) + chunk, bf),
            pltpu.VMEM(chunk, bf),
            pltpu.VMEM((3,) + piece, bf),
            pltpu.VMEM(piece, bf),
            pltpu.VMEM(piece, bf),
            dma((4, parts)), dma((4, parts)),
            dma((3, parts)), dma((3, parts)),
            dma((3, parts)), dma((3, parts)),
            dma((3, parts)), dma((3, parts)),
            dma((3, parts)), dma((3, parts)),
            dma((4, parts)), dma((4, parts)),
        ],
        compiler_params=pltpu.CompilerParams(
            collective_id=0, has_side_effects=True, vmem_limit_bytes=24 * 1024 * 1024
        ),
    )(owners, slots, scen_map, border, inverses)


def reduce_kernel(
    turned, shared, out,
    own, a_out, a_in, b_out, b_in, half_out, half_in,
    a_s, a_r, b_s, b_r, h_s, h_r,
):
    at = lax.axis_index("grp")
    zl = lax.rem(at, 2)
    y = lax.div(at, 2)
    core = lax.rem(lax.axis_index("col"), 2)
    way = 1 - 2 * core

    def ring(step):
        return lax.rem(y + step * way + 2 * Y, Y)

    fwd, back = ring(1) * 2 + zl, ring(-1) * 2 + zl
    mate = y * 2 + (1 - zl)
    panels = own.shape[0]
    greet([("grp", d) for d in (fwd, back, mate)])

    far, near = Y // 2, Y // 2 - 1
    sent = []
    ahead, behind, halves = {}, {}, {}

    def product(p):
        halves_of = [
            shared[p // 2, :, :, p % 2 * 2 + k].reshape(-1, LANE) for k in range(2)
        ]
        right = jnp.concatenate(halves_of, axis=1)
        whole = jnp.dot(turned[...], right, preferred_element_type=jnp.float32)
        own[p] = whole.reshape(own.shape[1:])

    def hop(p, t):
        term = own[p, ring(far - t)]
        if t > 0:
            ahead[p].wait_recv()
            term = term + a_in[p, t - 1].astype(jnp.float32)
        a_out[p, t] = term.astype(jnp.bfloat16)
        ahead[p] = remote(a_out.at[p, t], a_in.at[p, t], a_s.at[p, t], a_r.at[p, t], "grp", fwd)
        sent.append(ahead[p])
        if t < near:
            term = own[p, ring(t - near)]
            if t > 0:
                behind[p].wait_recv()
                term = term + b_in[p, t - 1].astype(jnp.float32)
            b_out[p, t] = term.astype(jnp.bfloat16)
            behind[p] = remote(b_out.at[p, t], b_in.at[p, t], b_s.at[p, t], b_r.at[p, t], "grp", back)
            sent.append(behind[p])

    def meet(p):
        behind[p].wait_recv()
        ahead[p].wait_recv()

        def total(z):
            return (
                own[p, y, z]
                + a_in[p, far - 1, z].astype(jnp.float32)
                + b_in[p, near - 1, z].astype(jnp.float32)
            )

        half_out[p] = total(1 - zl)
        halves[p] = remote(half_out.at[p], half_in.at[p], h_s.at[p], h_r.at[p], "grp", mate)
        sent.append(halves[p])
        out[p] = total(zl)

    def finish(p):
        halves[p].wait_recv()
        out[p] = out[p] + half_in[p]

    for u in range(panels + far + 1):
        if u < panels:
            product(u)
        for p in range(panels):
            t = u - p
            if 0 <= t < far:
                hop(p, t)
            elif t == far:
                meet(p)
            elif t == far + 1:
                finish(p)
    for copy in sent:
        copy.wait_send()


def reduce_over_groups(turned, shared):
    panels, width = 4, 2 * LANE
    rows = turned.shape[0] // (2 * Y)
    block = (2, rows, width)
    far, near = Y // 2, Y // 2 - 1
    f32, bf = jnp.float32, jnp.bfloat16
    dma = pltpu.SemaphoreType.DMA
    vm = pl.BlockSpec(memory_space=pltpu.VMEM)
    return pl.pallas_call(
        reduce_kernel,
        out_shape=jax.ShapeDtypeStruct((panels, rows, width), f32),
        in_specs=[vm, vm],
        out_specs=vm,
        scratch_shapes=[
            pltpu.VMEM((panels, Y) + block, f32),
            pltpu.VMEM((panels, far) + block, bf),
            pltpu.VMEM((panels, far) + block, bf),
            pltpu.VMEM((panels, near) + block, bf),
            pltpu.VMEM((panels, near) + block, bf),
            pltpu.VMEM((panels, rows, width), f32),
            pltpu.VMEM((panels, rows, width), f32),
            dma((panels, far)), dma((panels, far)),
            dma((panels, near)), dma((panels, near)),
            dma((panels,)), dma((panels,)),
        ],
        compiler_params=pltpu.CompilerParams(
            collective_id=1, has_side_effects=True, vmem_limit_bytes=24 * 1024 * 1024
        ),
    )(turned, shared)


def on_device(border, inverses, scen_map, owners, slots):
    shared, turned = share(owners, slots, scen_map, border, inverses)
    return reduce_over_groups(turned, shared)


def solution(mesh):
    return jax.shard_map(
        on_device,
        mesh=mesh,
        in_specs=(P("grp", None, "col"), P("grp", None, None), P("grp", None), P(), P()),
        out_specs=P(None, ("col", "grp"), None),
        check_vma=False,
    )
```

```python
import jax
import jax.numpy as jnp
from jax import lax
from jax.experimental import pallas as pl
from jax.experimental.pallas import tpu as pltpu
from jax.sharding import PartitionSpec as P

X = 4
ZH = 4
Y = 8
LANE = 128
TILE = 16
SHARE_REFS = 29


def greet(peers):
    barrier = pltpu.get_barrier_semaphore()
    for axis, peer in peers:
        pl.semaphore_signal(
            barrier, inc=1, device_id={axis: peer}, device_id_type=pl.DeviceIdType.MESH
        )
    pl.semaphore_wait(barrier, len(peers))


def remote(src, dst, send, recv, axis, peer):
    copy = pltpu.make_async_remote_copy(
        src_ref=src,
        dst_ref=dst,
        send_sem=send,
        recv_sem=recv,
        device_id={axis: peer},
        device_id_type=pl.DeviceIdType.MESH,
    )
    copy.start()
    return copy


def share(
    owners_at, slots_at, scen_map_at, border_at, inverses_at, full, turned, neighbours,
    owners, slots, scen_map, border, inverses, loads,
    marks, picked, pair_out, pair_in, x_out, x_own, x_in, z_sum, z_in, z_out, home,
    pair_s, pair_r, xs, xr, zs, zr, zgs, zgr, xgs, xgr, bs, br,
):
    fetch = [
        pltpu.make_async_copy(src, dst, loads.at[k])
        for k, (src, dst) in enumerate((
            (owners_at, owners), (slots_at, slots), (scen_map_at, scen_map),
            (border_at, border), (inverses_at, inverses),
        ))
    ]
    for copy in fetch:
        copy.start()
    at = lax.axis_index("col")
    core = lax.rem(at, 2)
    zh = lax.rem(lax.div(at, 2), ZH)
    x = lax.div(at, 2 * ZH)
    way = 1 - 2 * core
    other = 1 - core

    def col(xx, zz, cc):
        return (xx * ZH + zz) * 2 + cc

    def flag(left, right):
        same = jnp.full((TILE, LANE), left, jnp.int32) == jnp.full((TILE, LANE), right, jnp.int32)
        return jnp.where(same, 1.0, 0.0)

    scen, depth, _ = border.shape
    parts = depth // LANE
    tiles = LANE // TILE
    def panel(cc, s, r, q):
        total = None
        for k in range(3):
            start = k * 2 * LANE + (q % 2) * LANE
            block = border[s, r * LANE:(r + 1) * LANE, start:start + LANE]
            block = block.reshape(tiles, TILE, LANE)
            term = block * marks[2 * cc + q // 2, k][None]
            total = term if total is None else total + term
        return total.reshape(LANE, LANE)

    def turn(s):
        turned[:, s * depth:(s + 1) * depth] = border[s].T

    xa, xb, xf = lax.rem(x + way + X, X), lax.rem(x - way + X, X), lax.rem(x + 2, X)
    za, zb, zf = lax.rem(zh + way + ZH, ZH), lax.rem(zh - way + ZH, ZH), lax.rem(zh + 2, ZH)
    partner = col(x, zh, other)
    x_fwd, x_back = col(xa, zh, core), col(xb, zh, core)
    z_fwd, z_back = col(x, za, core), col(x, zb, core)
    for copy in fetch[:3]:
        copy.wait()
    for p in range(owners.shape[0]):
        for k in range(3):
            marks[p, k] = (flag(owners[p], at) * flag(slots[p], k)).astype(jnp.bfloat16)

    greet([("col", d) for d in (partner, x_fwd, x_back, z_fwd, z_back)] + neighbours)
    fetch[3].wait()

    order = range(parts)
    sends = []

    def send(*args):
        copy = remote(*args)
        sends.append(copy)
        return copy

    pair = {}
    for k, s in enumerate((xf, xa, xb, x)):
        for r in order:
            for q in range(ZH):
                pair_out[k, r, q] = panel(other, s, r, q)
            pair[k, r] = send(
                pair_out.at[k, r], pair_in.at[s, r], pair_s.at[k, r], pair_r.at[k, r], "col", partner
            )

    def joined(k, s, r, q):
        return panel(core, s, r, q) + pair_in[s, r, q]

    c = {}
    for k, s, peer in ((0, xf, x_fwd), (1, xb, x_back)):
        for r in order:
            pair[k, r].wait_recv()
            for q in range(ZH):
                x_out[k, r, q] = joined(k, s, r, q)
            c[k, r] = send(x_out.at[k, r], x_in.at[k, r], xs.at[k, r], xr.at[k, r], "col", peer)
    for r in order:
        pair[2, r].wait_recv()
        for q in range(ZH):
            x_own[0, r, q] = joined(2, xa, r, q)
    turn(0)
    for r in order:
        c[0, r].wait_recv()
        for q in range(ZH):
            x_out[2, r, q] = x_own[0, r, q] + x_in[0, r, q]
        c[2, r] = send(x_out.at[2, r], x_in.at[2, r], xs.at[2, r], xr.at[2, r], "col", x_fwd)
    fetch[4].wait()
    for lane in range(0, depth, LANE):
        for r in order:
            total = None
            for k in range(scen):
                mark = flag(scen_map[0, x], k).astype(jnp.bfloat16)
                block = inverses[k, r * LANE:(r + 1) * LANE, lane:lane + LANE]
                term = block.reshape(tiles, TILE, LANE) * mark[None]
                total = term if total is None else total + term
            picked[r * LANE:(r + 1) * LANE, lane:lane + LANE] = total.reshape(LANE, LANE)
    for r in order:
        pair[3, r].wait_recv()
        c[1, r].wait_recv()
        for q in range(ZH):
            x_own[1, r, q] = joined(3, x, r, q) + x_in[1, r, q]
    turn(1)

    d = {}

    def relay(r):
        d[0, r].wait_recv()
        z_out[r] = z_sum[r, za] + z_in[0, r]
        d[2, r] = send(z_out.at[r], z_in.at[2, r], zs.at[2, r], zr.at[2, r], "col", z_fwd)

    for r in order:
        c[2, r].wait_recv()
        for q in range(ZH):
            z_sum[r, q] = x_own[1, r, q] + x_in[2, r, q]
        d[0, r] = send(z_sum.at[r, zf], z_in.at[0, r], zs.at[0, r], zr.at[0, r], "col", z_fwd)
        d[1, r] = send(z_sum.at[r, zb], z_in.at[1, r], zs.at[1, r], zr.at[1, r], "col", z_back)
        if r > 0:
            relay(r - 1)
    relay(parts - 1)
    result = None
    for r in order:
        d[1, r].wait_recv()
        part = z_sum[r, zh] + z_in[1, r]
        d[2, r].wait_recv()
        part = part + z_in[2, r]
        term = jnp.dot(
            picked[:, r * LANE:(r + 1) * LANE], part, preferred_element_type=jnp.float32
        )
        result = term if result is None else result + term

    e = {}
    for r in order:
        home[r] = result[r * LANE:(r + 1) * LANE].astype(jnp.bfloat16)
        for k, peer in ((0, z_fwd), (1, z_back)):
            e[k, r] = send(
                home.at[r], full.at[core, x, r, zh], zgs.at[k, r], zgr.at[k, r], "col", peer
            )
        full[core, x, r, zh] = home[r]

    def pass_on(k, s, r, sent, got, axis, peer):
        return send(full.at[core, s, r], full.at[core, s, r], sent.at[k, r], got.at[k, r], axis, peer)

    for r in order:
        e[0, r].wait_recv()
        held = full.at[core, x, r, zb]
        e[2, r] = send(held, held, zgs.at[2, r], zgr.at[2, r], "col", z_fwd)
    g, h = {}, {}
    for r in order:
        e[1, r].wait_recv()
        e[2, r].wait_recv()
        g[0, r] = pass_on(0, x, r, xgs, xgr, "col", x_fwd)
        g[1, r] = pass_on(1, x, r, xgs, xgr, "col", x_back)
        h[0, r] = pass_on(0, x, r, bs, br, "col", partner)
    turn(2)
    for r in order:
        g[0, r].wait_recv()
        g[2, r] = pass_on(2, xb, r, xgs, xgr, "col", x_fwd)
        h[1, r] = pass_on(1, xb, r, bs, br, "col", partner)
    turn(3)
    for r in order:
        g[1, r].wait_recv()
        h[2, r] = pass_on(2, xa, r, bs, br, "col", partner)
    for r in order:
        g[2, r].wait_recv()
        h[3, r] = pass_on(3, xf, r, bs, br, "col", partner)
    for copy in h.values():
        copy.wait_recv()
    return sends


def group_place():
    at = lax.axis_index("grp")
    zl = lax.rem(at, 2)
    y = lax.div(at, 2)
    core = lax.rem(lax.axis_index("col"), 2)
    way = 1 - 2 * core

    def ring(step):
        return lax.rem(y + step * way + 2 * Y, Y)

    fwd, back = ring(1) * 2 + zl, ring(-1) * 2 + zl
    mate = y * 2 + (1 - zl)
    return y, zl, ring, (fwd, back, mate)


def reduce(
    turned, shared, out, sent,
    own, a_out, a_in, b_out, b_in, half_out, half_in,
    a_s, a_r, b_s, b_r, h_s, h_r,
):
    y, zl, ring, (fwd, back, mate) = group_place()
    panels = own.shape[0]

    far, near = Y // 2, Y // 2 - 1
    ahead, behind, halves = {}, {}, {}

    def product(p):
        halves_of = [
            shared[p // 2, :, :, p % 2 * 2 + k].reshape(-1, LANE) for k in range(2)
        ]
        right = jnp.concatenate(halves_of, axis=1)
        whole = jnp.dot(turned[...], right, preferred_element_type=jnp.float32)
        own[p] = whole.reshape(own.shape[1:])

    def hop(p, t):
        term = own[p, ring(far - t)]
        if t > 0:
            ahead[p].wait_recv()
            term = term + a_in[p, t - 1].astype(jnp.float32)
        a_out[p, t] = term.astype(jnp.bfloat16)
        ahead[p] = remote(a_out.at[p, t], a_in.at[p, t], a_s.at[p, t], a_r.at[p, t], "grp", fwd)
        sent.append(ahead[p])
        if t < near:
            term = own[p, ring(t - near)]
            if t > 0:
                behind[p].wait_recv()
                term = term + b_in[p, t - 1].astype(jnp.float32)
            b_out[p, t] = term.astype(jnp.bfloat16)
            behind[p] = remote(b_out.at[p, t], b_in.at[p, t], b_s.at[p, t], b_r.at[p, t], "grp", back)
            sent.append(behind[p])

    def meet(p):
        behind[p].wait_recv()
        ahead[p].wait_recv()

        def total(z):
            return (
                own[p, y, z]
                + a_in[p, far - 1, z].astype(jnp.float32)
                + b_in[p, near - 1, z].astype(jnp.float32)
            )

        half_out[p] = total(1 - zl)
        halves[p] = remote(half_out.at[p], half_in.at[p], h_s.at[p], h_r.at[p], "grp", mate)
        sent.append(halves[p])
        out[p] = total(zl)

    def finish(p):
        halves[p].wait_recv()
        out[p] = out[p] + half_in[p]

    for u in range(panels + far + 1):
        if u < panels:
            product(u)
        for p in reversed(range(panels)):
            t = u - p
            if 0 <= t < far:
                hop(p, t)
            elif t == far:
                meet(p)
            elif t == far + 1:
                finish(p)


def kernel(owners, slots, scen_map, border, inverses, out, full, turned, *scratch):
    _, _, _, peers = group_place()
    first = scratch[:SHARE_REFS]
    sends = share(
        owners, slots, scen_map, border, inverses, full, turned,
        [("grp", d) for d in peers], *first
    )
    reduce(turned, full, out, sends, *scratch[SHARE_REFS:])
    for copy in sends:
        copy.wait_send()


def schur(owners, slots, scen_map, border, inverses):
    scen, depth, cols = border.shape
    parts = depth // LANE
    piece = (parts, LANE, LANE)
    chunk = (parts, ZH, LANE, LANE)
    panels, width = owners.shape[0], 2 * LANE
    rows = cols // (2 * Y)
    block = (2, rows, width)
    far, near = Y // 2, Y // 2 - 1
    f32, bf = jnp.float32, jnp.bfloat16
    dma = pltpu.SemaphoreType.DMA
    hbm = pl.BlockSpec(memory_space=pltpu.HBM)
    return pl.pallas_call(
        kernel,
        out_shape=jax.ShapeDtypeStruct((panels, rows, width), f32),
        in_specs=[hbm] * 5,
        out_specs=pl.BlockSpec(memory_space=pltpu.VMEM),
        scratch_shapes=[
            pltpu.VMEM((2, X) + chunk, bf),
            pltpu.VMEM((cols, scen * depth), bf),
            pltpu.SMEM(owners.shape, jnp.int32),
            pltpu.SMEM(slots.shape, jnp.int32),
            pltpu.SMEM(scen_map.shape, jnp.int32),
            pltpu.VMEM(border.shape, bf),
            pltpu.VMEM(inverses.shape, bf),
            dma((5,)),
            pltpu.VMEM((4, 3, TILE, LANE), bf),
            pltpu.VMEM((depth, depth), bf),
            pltpu.VMEM((X,) + chunk, bf),
            pltpu.VMEM((X,) + chunk, bf),
            pltpu.VMEM((3,) + chunk, bf),
            pltpu.VMEM((2,) + chunk, bf),
            pltpu.VMEM((3,) + chunk, bf),
            pltpu.VMEM(chunk, bf),
            pltpu.VMEM((3,) + piece, bf),
            pltpu.VMEM(piece, bf),
            pltpu.VMEM(piece, bf),
            dma((4, parts)), dma((4, parts)),
            dma((3, parts)), dma((3, parts)),
            dma((3, parts)), dma((3, parts)),
            dma((3, parts)), dma((3, parts)),
            dma((3, parts)), dma((3, parts)),
            dma((4, parts)), dma((4, parts)),
            pltpu.VMEM((panels, Y) + block, f32),
            pltpu.VMEM((panels, far) + block, bf),
            pltpu.VMEM((panels, far) + block, bf),
            pltpu.VMEM((panels, near) + block, bf),
            pltpu.VMEM((panels, near) + block, bf),
            pltpu.VMEM((panels, rows, width), f32),
            pltpu.VMEM((panels, rows, width), f32),
            dma((panels, far)), dma((panels, far)),
            dma((panels, near)), dma((panels, near)),
            dma((panels,)), dma((panels,)),
        ],
        compiler_params=pltpu.CompilerParams(
            collective_id=0, has_side_effects=True, vmem_limit_bytes=64000 * 1024
        ),
    )(owners, slots, scen_map, border, inverses)


def on_device(border, inverses, scen_map, owners, slots):
    return schur(owners, slots, scen_map, border, inverses)


def solution(mesh):
    return jax.shard_map(
        on_device,
        mesh=mesh,
        in_specs=(P("grp", None, "col"), P("grp", None, None), P("grp", None), P(), P()),
        out_specs=P(None, ("col", "grp"), None),
        check_vma=False,
    )
```

```python
import jax
import jax.numpy as jnp
from jax import lax
from jax.experimental import pallas as pl
from jax.experimental.pallas import tpu as pltpu
from jax.sharding import PartitionSpec as P

X = 4
ZH = 4
Y = 8
LANE = 128
TILE = 16
SHARE_REFS = 29


def greet(peers):
    barrier = pltpu.get_barrier_semaphore()
    for axis, peer in peers:
        pl.semaphore_signal(
            barrier, inc=1, device_id={axis: peer}, device_id_type=pl.DeviceIdType.MESH
        )
    pl.semaphore_wait(barrier, len(peers))


def remote(src, dst, send, recv, axis, peer):
    copy = pltpu.make_async_remote_copy(
        src_ref=src,
        dst_ref=dst,
        send_sem=send,
        recv_sem=recv,
        device_id={axis: peer},
        device_id_type=pl.DeviceIdType.MESH,
    )
    copy.start()
    return copy


def share(
    owners_at, slots_at, scen_map_at, border_at, inverses_at, full, turned, neighbours,
    owners, slots, scen_map, border, inverses, loads,
    marks, picked, pair_out, pair_in, x_out, x_own, x_in, z_sum, z_in, z_out, home,
    pair_s, pair_r, xs, xr, zs, zr, zgs, zgr, xgs, xgr, bs, br,
):
    fetch = [
        pltpu.make_async_copy(src, dst, loads.at[k])
        for k, (src, dst) in enumerate((
            (owners_at, owners), (slots_at, slots), (scen_map_at, scen_map),
            (border_at, border), (inverses_at, inverses),
        ))
    ]
    for copy in fetch:
        copy.start()
    at = lax.axis_index("col")
    core = lax.rem(at, 2)
    zh = lax.rem(lax.div(at, 2), ZH)
    x = lax.div(at, 2 * ZH)
    way = 1 - 2 * core
    other = 1 - core

    def col(xx, zz, cc):
        return (xx * ZH + zz) * 2 + cc

    def flag(left, right):
        same = jnp.full((TILE, LANE), left, jnp.int32) == jnp.full((TILE, LANE), right, jnp.int32)
        return jnp.where(same, 1.0, 0.0)

    scen, depth, _ = border.shape
    parts = depth // LANE
    tiles = LANE // TILE
    def panel(cc, s, r, q):
        total = None
        for k in range(3):
            start = k * 2 * LANE + (q % 2) * LANE
            block = border[s, r * LANE:(r + 1) * LANE, start:start + LANE]
            block = block.reshape(tiles, TILE, LANE)
            term = block * marks[2 * cc + q // 2, k][None]
            total = term if total is None else total + term
        return total.reshape(LANE, LANE)

    def turn(s):
        turned[:, s * depth:(s + 1) * depth] = border[s].T

    xa, xb, xf = lax.rem(x + way + X, X), lax.rem(x - way + X, X), lax.rem(x + 2, X)
    za, zb, zf = lax.rem(zh + way + ZH, ZH), lax.rem(zh - way + ZH, ZH), lax.rem(zh + 2, ZH)
    partner = col(x, zh, other)
    x_fwd, x_back = col(xa, zh, core), col(xb, zh, core)
    z_fwd, z_back = col(x, za, core), col(x, zb, core)
    for copy in fetch[:3]:
        copy.wait()
    for p in range(owners.shape[0]):
        for k in range(3):
            marks[p, k] = (flag(owners[p], at) * flag(slots[p], k)).astype(jnp.bfloat16)

    greet([("col", d) for d in (partner, x_fwd, x_back, z_fwd, z_back)] + neighbours)
    fetch[3].wait()

    order = range(parts)
    sends = []

    def send(*args):
        copy = remote(*args)
        sends.append(copy)
        return copy

    pair = {}
    for k, s in enumerate((xf, xa, xb, x)):
        for r in order:
            for q in range(ZH):
                pair_out[k, r, q] = panel(other, s, r, q)
            pair[k, r] = send(
                pair_out.at[k, r], pair_in.at[s, r], pair_s.at[k, r], pair_r.at[k, r], "col", partner
            )

    def joined(k, s, r, q):
        return panel(core, s, r, q) + pair_in[s, r, q]

    c = {}
    for k, s, peer in ((0, xf, x_fwd), (1, xb, x_back)):
        for r in order:
            pair[k, r].wait_recv()
            for q in range(ZH):
                x_out[k, r, q] = joined(k, s, r, q)
            c[k, r] = send(x_out.at[k, r], x_in.at[k, r], xs.at[k, r], xr.at[k, r], "col", peer)
    for r in order:
        pair[2, r].wait_recv()
        for q in range(ZH):
            x_own[0, r, q] = joined(2, xa, r, q)
    turn(0)
    for r in order:
        c[0, r].wait_recv()
        for q in range(ZH):
            x_out[2, r, q] = x_own[0, r, q] + x_in[0, r, q]
        c[2, r] = send(x_out.at[2, r], x_in.at[2, r], xs.at[2, r], xr.at[2, r], "col", x_fwd)
    fetch[4].wait()
    for lane in range(0, depth, LANE):
        for r in order:
            total = None
            for k in range(scen):
                mark = flag(scen_map[0, x], k).astype(jnp.bfloat16)
                block = inverses[k, r * LANE:(r + 1) * LANE, lane:lane + LANE]
                term = block.reshape(tiles, TILE, LANE) * mark[None]
                total = term if total is None else total + term
            picked[r * LANE:(r + 1) * LANE, lane:lane + LANE] = total.reshape(LANE, LANE)
    for r in order:
        pair[3, r].wait_recv()
        c[1, r].wait_recv()
        for q in range(ZH):
            x_own[1, r, q] = joined(3, x, r, q) + x_in[1, r, q]
    turn(1)

    d = {}

    def relay(r):
        d[0, r].wait_recv()
        z_out[r] = z_sum[r, za] + z_in[0, r]
        d[2, r] = send(z_out.at[r], z_in.at[2, r], zs.at[2, r], zr.at[2, r], "col", z_fwd)

    for r in order:
        c[2, r].wait_recv()
        for q in range(ZH):
            z_sum[r, q] = x_own[1, r, q] + x_in[2, r, q]
        d[0, r] = send(z_sum.at[r, zf], z_in.at[0, r], zs.at[0, r], zr.at[0, r], "col", z_fwd)
        d[1, r] = send(z_sum.at[r, zb], z_in.at[1, r], zs.at[1, r], zr.at[1, r], "col", z_back)
        if r > 0:
            relay(r - 1)
    relay(parts - 1)
    result = None
    for r in order:
        d[1, r].wait_recv()
        part = z_sum[r, zh] + z_in[1, r]
        d[2, r].wait_recv()
        part = part + z_in[2, r]
        term = jnp.dot(
            picked[:, r * LANE:(r + 1) * LANE], part, preferred_element_type=jnp.float32
        )
        result = term if result is None else result + term

    e = {}
    for r in order:
        home[r] = result[r * LANE:(r + 1) * LANE].astype(jnp.bfloat16)
        for k, peer in ((0, z_fwd), (1, z_back)):
            e[k, r] = send(
                home.at[r], full.at[core, x, r, zh], zgs.at[k, r], zgr.at[k, r], "col", peer
            )
        full[core, x, r, zh] = home[r]

    g, h = {}, {}

    def pass_on(kept, k, s, i, r, sent, got, peer):
        held = full.at[core, s, r, 2 * i:2 * i + 2]
        kept[k, i, r] = send(held, held, sent.at[k, i, r], got.at[k, i, r], "col", peer)

    def to_partner(k, s, i, r):
        pass_on(h, k, s, i, r, bs, br, partner)

    def spread_own(i, r):
        pass_on(g, 0, x, i, r, xgs, xgr, x_fwd)
        pass_on(g, 1, x, i, r, xgs, xgr, x_back)
        to_partner(0, x, i, r)

    def take_back(i):
        for r in order:
            g[0, i, r].wait_recv()
            pass_on(g, 2, xb, i, r, xgs, xgr, x_fwd)
            to_partner(1, xb, i, r)

    def take_fwd(i):
        for r in order:
            g[1, i, r].wait_recv()
            to_partner(2, xa, i, r)

    def take_far(i):
        for r in order:
            g[2, i, r].wait_recv()
            to_partner(3, xf, i, r)
        for k in range(X):
            for r in order:
                h[k, i, r].wait_recv()

    turn(2)
    for r in order:
        e[0, r].wait_recv()
        held = full.at[core, x, r, zb]
        e[2, r] = send(held, held, zgs.at[2, r], zgr.at[2, r], "col", z_fwd)
    for r in order:
        e[1, r].wait_recv()
        e[2, r].wait_recv()
        spread_own(0, r)
    take_back(0)
    for r in order:
        spread_own(1, r)
    turn(3)
    take_fwd(0)
    take_far(0)
    return sends, {1: take_back, 2: take_fwd, 3: take_far}


def group_place():
    at = lax.axis_index("grp")
    zl = lax.rem(at, 2)
    y = lax.div(at, 2)
    core = lax.rem(lax.axis_index("col"), 2)
    way = 1 - 2 * core

    def ring(step):
        return lax.rem(y + step * way + 2 * Y, Y)

    fwd, back = ring(1) * 2 + zl, ring(-1) * 2 + zl
    mate = y * 2 + (1 - zl)
    return y, zl, ring, (fwd, back, mate)


def reduce(
    turned, shared, out, sent, before,
    own, a_out, a_in, b_out, b_in, half_out, half_in,
    a_s, a_r, b_s, b_r, h_s, h_r,
):
    y, zl, ring, (fwd, back, mate) = group_place()
    panels = own.shape[0]

    far, near = Y // 2, Y // 2 - 1
    ahead, behind, halves = {}, {}, {}

    def product(p):
        halves_of = [
            shared[p // 2, :, :, p % 2 * 2 + k].reshape(-1, LANE) for k in range(2)
        ]
        right = jnp.concatenate(halves_of, axis=1)
        whole = jnp.dot(turned[...], right, preferred_element_type=jnp.float32)
        own[p] = whole.reshape(own.shape[1:])

    def hop(p, t):
        term = own[p, ring(far - t)]
        if t > 0:
            ahead[p].wait_recv()
            term = term + a_in[p, t - 1].astype(jnp.float32)
        a_out[p, t] = term.astype(jnp.bfloat16)
        ahead[p] = remote(a_out.at[p, t], a_in.at[p, t], a_s.at[p, t], a_r.at[p, t], "grp", fwd)
        sent.append(ahead[p])
        if t < near:
            term = own[p, ring(t - near)]
            if t > 0:
                behind[p].wait_recv()
                term = term + b_in[p, t - 1].astype(jnp.float32)
            b_out[p, t] = term.astype(jnp.bfloat16)
            behind[p] = remote(b_out.at[p, t], b_in.at[p, t], b_s.at[p, t], b_r.at[p, t], "grp", back)
            sent.append(behind[p])

    def meet(p):
        behind[p].wait_recv()
        ahead[p].wait_recv()

        def total(z):
            return (
                own[p, y, z]
                + a_in[p, far - 1, z].astype(jnp.float32)
                + b_in[p, near - 1, z].astype(jnp.float32)
            )

        half_out[p] = total(1 - zl)
        halves[p] = remote(half_out.at[p], half_in.at[p], h_s.at[p], h_r.at[p], "grp", mate)
        sent.append(halves[p])
        out[p] = total(zl)

    def finish(p):
        halves[p].wait_recv()
        out[p] = out[p] + half_in[p]

    starts = {0: 0, 2: 1, 1: 3, 3: 4}
    for u in range(max(starts.values()) + far + 2):
        if u in before:
            before[u](1)
        for p in reversed((0, 2, 1, 3)):
            t = u - starts[p]
            if t == 0:
                product(p)
            if 0 <= t < far:
                hop(p, t)
            elif t == far:
                meet(p)
            elif t == far + 1:
                finish(p)


def kernel(owners, slots, scen_map, border, inverses, out, full, turned, *scratch):
    _, _, _, peers = group_place()
    first = scratch[:SHARE_REFS]
    sends, later = share(
        owners, slots, scen_map, border, inverses, full, turned,
        [("grp", d) for d in peers], *first
    )
    reduce(turned, full, out, sends, later, *scratch[SHARE_REFS:])
    for copy in sends:
        copy.wait_send()


def schur(owners, slots, scen_map, border, inverses):
    scen, depth, cols = border.shape
    parts = depth // LANE
    piece = (parts, LANE, LANE)
    chunk = (parts, ZH, LANE, LANE)
    panels, width = owners.shape[0], 2 * LANE
    rows = cols // (2 * Y)
    block = (2, rows, width)
    far, near = Y // 2, Y // 2 - 1
    f32, bf = jnp.float32, jnp.bfloat16
    dma = pltpu.SemaphoreType.DMA
    hbm = pl.BlockSpec(memory_space=pltpu.HBM)
    return pl.pallas_call(
        kernel,
        out_shape=jax.ShapeDtypeStruct((panels, rows, width), f32),
        in_specs=[hbm] * 5,
        out_specs=pl.BlockSpec(memory_space=pltpu.VMEM),
        scratch_shapes=[
            pltpu.VMEM((2, X) + chunk, bf),
            pltpu.VMEM((cols, scen * depth), bf),
            pltpu.SMEM(owners.shape, jnp.int32),
            pltpu.SMEM(slots.shape, jnp.int32),
            pltpu.SMEM(scen_map.shape, jnp.int32),
            pltpu.VMEM(border.shape, bf),
            pltpu.VMEM(inverses.shape, bf),
            dma((5,)),
            pltpu.VMEM((4, 3, TILE, LANE), bf),
            pltpu.VMEM((depth, depth), bf),
            pltpu.VMEM((X,) + chunk, bf),
            pltpu.VMEM((X,) + chunk, bf),
            pltpu.VMEM((3,) + chunk, bf),
            pltpu.VMEM((2,) + chunk, bf),
            pltpu.VMEM((3,) + chunk, bf),
            pltpu.VMEM(chunk, bf),
            pltpu.VMEM((3,) + piece, bf),
            pltpu.VMEM(piece, bf),
            pltpu.VMEM(piece, bf),
            dma((4, parts)), dma((4, parts)),
            dma((3, parts)), dma((3, parts)),
            dma((3, parts)), dma((3, parts)),
            dma((3, parts)), dma((3, parts)),
            dma((3, 2, parts)), dma((3, 2, parts)),
            dma((4, 2, parts)), dma((4, 2, parts)),
            pltpu.VMEM((panels, Y) + block, f32),
            pltpu.VMEM((panels, far) + block, bf),
            pltpu.VMEM((panels, far) + block, bf),
            pltpu.VMEM((panels, near) + block, bf),
            pltpu.VMEM((panels, near) + block, bf),
            pltpu.VMEM((panels, rows, width), f32),
            pltpu.VMEM((panels, rows, width), f32),
            dma((panels, far)), dma((panels, far)),
            dma((panels, near)), dma((panels, near)),
            dma((panels,)), dma((panels,)),
        ],
        compiler_params=pltpu.CompilerParams(
            collective_id=0, has_side_effects=True, vmem_limit_bytes=64000 * 1024
        ),
    )(owners, slots, scen_map, border, inverses)


def on_device(border, inverses, scen_map, owners, slots):
    return schur(owners, slots, scen_map, border, inverses)


def solution(mesh):
    return jax.shard_map(
        on_device,
        mesh=mesh,
        in_specs=(P("grp", None, "col"), P("grp", None, None), P("grp", None), P(), P()),
        out_specs=P(None, ("col", "grp"), None),
        check_vma=False,
    )
```

```python
import jax
import jax.numpy as jnp
from jax import lax
from jax.experimental import pallas as pl
from jax.experimental.pallas import tpu as pltpu
from jax.sharding import PartitionSpec as P

X = 4
ZH = 4
Y = 8
LANE = 128
TILE = 16
SHARE_REFS = 29


def greet(peers):
    barrier = pltpu.get_barrier_semaphore()
    for axis, peer in peers:
        pl.semaphore_signal(
            barrier, inc=1, device_id={axis: peer}, device_id_type=pl.DeviceIdType.MESH
        )
    pl.semaphore_wait(barrier, len(peers))


def remote(src, dst, send, recv, axis, peer):
    copy = pltpu.make_async_remote_copy(
        src_ref=src,
        dst_ref=dst,
        send_sem=send,
        recv_sem=recv,
        device_id={axis: peer},
        device_id_type=pl.DeviceIdType.MESH,
    )
    copy.start()
    return copy


def share(
    owners_at, slots_at, scen_map_at, border_at, inverses_at, full, turned, neighbours,
    owners, slots, scen_map, border, inverses, loads,
    marks, picked, pair_out, pair_in, x_out, x_own, x_in, z_sum, z_in, z_out, home,
    pair_s, pair_r, xs, xr, zs, zr, zgs, zgr, xgs, xgr, bs, br,
):
    fetch = [
        pltpu.make_async_copy(src, dst, loads.at[k])
        for k, (src, dst) in enumerate((
            (owners_at, owners), (slots_at, slots), (scen_map_at, scen_map),
            (border_at, border), (inverses_at, inverses),
        ))
    ]
    for copy in fetch:
        copy.start()
    at = lax.axis_index("col")
    core = lax.rem(at, 2)
    zh = lax.rem(lax.div(at, 2), ZH)
    x = lax.div(at, 2 * ZH)
    way = 1 - 2 * core
    other = 1 - core

    def col(xx, zz, cc):
        return (xx * ZH + zz) * 2 + cc

    def flag(left, right):
        same = jnp.full((TILE, LANE), left, jnp.int32) == jnp.full((TILE, LANE), right, jnp.int32)
        return jnp.where(same, 1.0, 0.0)

    scen, depth, _ = border.shape
    parts = depth // LANE
    tiles = LANE // TILE
    def panel(cc, s, r, q):
        total = None
        for k in range(3):
            start = k * 2 * LANE + (q % 2) * LANE
            block = border[s, r * LANE:(r + 1) * LANE, start:start + LANE]
            block = block.reshape(tiles, TILE, LANE)
            term = block * marks[2 * cc + q // 2, k][None]
            total = term if total is None else total + term
        return total.reshape(LANE, LANE)

    def turn(s):
        turned[:, s * depth:(s + 1) * depth] = border[s].T

    xa, xb, xf = lax.rem(x + way + X, X), lax.rem(x - way + X, X), lax.rem(x + 2, X)
    za, zb, zf = lax.rem(zh + way + ZH, ZH), lax.rem(zh - way + ZH, ZH), lax.rem(zh + 2, ZH)
    partner = col(x, zh, other)
    x_fwd, x_back = col(xa, zh, core), col(xb, zh, core)
    z_fwd, z_back = col(x, za, core), col(x, zb, core)
    for copy in fetch[:3]:
        copy.wait()
    for p in range(owners.shape[0]):
        for k in range(3):
            marks[p, k] = (flag(owners[p], at) * flag(slots[p], k)).astype(jnp.bfloat16)

    greet([("col", d) for d in (partner, x_fwd, x_back, z_fwd, z_back)] + neighbours)
    fetch[3].wait()

    order = range(parts)
    sends = []

    def send(*args):
        copy = remote(*args)
        sends.append(copy)
        return copy

    pair = {}

    def give(k, s):
        for r in order:
            for q in range(ZH):
                pair_out[k, r, q] = panel(other, s, r, q)
            pair[k, r] = send(
                pair_out.at[k, r], pair_in.at[s, r], pair_s.at[k, r], pair_r.at[k, r], "col", partner
            )

    def joined(k, s, r, q):
        return panel(core, s, r, q) + pair_in[s, r, q]

    c = {}

    def take(k, s, peer):
        for r in order:
            pair[k, r].wait_recv()
            for q in range(ZH):
                x_out[k, r, q] = joined(k, s, r, q)
            c[k, r] = send(x_out.at[k, r], x_in.at[k, r], xs.at[k, r], xr.at[k, r], "col", peer)

    give(0, xf)
    give(1, xa)
    take(0, xf, x_fwd)
    give(2, xb)
    take(1, xb, x_back)
    give(3, x)
    for r in order:
        pair[2, r].wait_recv()
        for q in range(ZH):
            x_own[0, r, q] = joined(2, xa, r, q)
    turn(0)
    for r in order:
        c[0, r].wait_recv()
        for q in range(ZH):
            x_out[2, r, q] = x_own[0, r, q] + x_in[0, r, q]
        c[2, r] = send(x_out.at[2, r], x_in.at[2, r], xs.at[2, r], xr.at[2, r], "col", x_fwd)
    fetch[4].wait()
    for lane in range(0, depth, LANE):
        for r in order:
            total = None
            for k in range(scen):
                mark = flag(scen_map[0, x], k).astype(jnp.bfloat16)
                block = inverses[k, r * LANE:(r + 1) * LANE, lane:lane + LANE]
                term = block.reshape(tiles, TILE, LANE) * mark[None]
                total = term if total is None else total + term
            picked[r * LANE:(r + 1) * LANE, lane:lane + LANE] = total.reshape(LANE, LANE)
    for r in order:
        pair[3, r].wait_recv()
        c[1, r].wait_recv()
        for q in range(ZH):
            x_own[1, r, q] = joined(3, x, r, q) + x_in[1, r, q]
    turn(1)

    d = {}

    def relay(r):
        d[0, r].wait_recv()
        z_out[r] = z_sum[r, za] + z_in[0, r]
        d[2, r] = send(z_out.at[r], z_in.at[2, r], zs.at[2, r], zr.at[2, r], "col", z_fwd)

    for r in order:
        c[2, r].wait_recv()
        for q in range(ZH):
            z_sum[r, q] = x_own[1, r, q] + x_in[2, r, q]
        d[0, r] = send(z_sum.at[r, zf], z_in.at[0, r], zs.at[0, r], zr.at[0, r], "col", z_fwd)
        d[1, r] = send(z_sum.at[r, zb], z_in.at[1, r], zs.at[1, r], zr.at[1, r], "col", z_back)
        if r > 0:
            relay(r - 1)
    relay(parts - 1)
    result = None
    for r in order:
        d[1, r].wait_recv()
        part = z_sum[r, zh] + z_in[1, r]
        d[2, r].wait_recv()
        part = part + z_in[2, r]
        term = jnp.dot(
            picked[:, r * LANE:(r + 1) * LANE], part, preferred_element_type=jnp.float32
        )
        result = term if result is None else result + term

    e = {}
    for r in order:
        home[r] = result[r * LANE:(r + 1) * LANE].astype(jnp.bfloat16)
        for k, peer in ((0, z_fwd), (1, z_back)):
            e[k, r] = send(
                home.at[r], full.at[core, x, r, zh], zgs.at[k, r], zgr.at[k, r], "col", peer
            )
        full[core, x, r, zh] = home[r]

    def pass_on(k, s, r, sent, got, axis, peer):
        return send(full.at[core, s, r], full.at[core, s, r], sent.at[k, r], got.at[k, r], axis, peer)

    turn(2)
    for r in order:
        e[0, r].wait_recv()
        held = full.at[core, x, r, zb]
        e[2, r] = send(held, held, zgs.at[2, r], zgr.at[2, r], "col", z_fwd)
    g, h = {}, {}
    for r in order:
        e[1, r].wait_recv()
        e[2, r].wait_recv()
        g[0, r] = pass_on(0, x, r, xgs, xgr, "col", x_fwd)
        g[1, r] = pass_on(1, x, r, xgs, xgr, "col", x_back)
        h[0, r] = pass_on(0, x, r, bs, br, "col", partner)
    for r in order:
        g[0, r].wait_recv()
        g[2, r] = pass_on(2, xb, r, xgs, xgr, "col", x_fwd)
        h[1, r] = pass_on(1, xb, r, bs, br, "col", partner)
    turn(3)
    for r in order:
        g[1, r].wait_recv()
        h[2, r] = pass_on(2, xa, r, bs, br, "col", partner)
    for r in order:
        g[2, r].wait_recv()
        h[3, r] = pass_on(3, xf, r, bs, br, "col", partner)
    for copy in h.values():
        copy.wait_recv()
    return sends


def group_place():
    at = lax.axis_index("grp")
    zl = lax.rem(at, 2)
    y = lax.div(at, 2)
    core = lax.rem(lax.axis_index("col"), 2)
    way = 1 - 2 * core

    def ring(step):
        return lax.rem(y + step * way + 2 * Y, Y)

    fwd, back = ring(1) * 2 + zl, ring(-1) * 2 + zl
    mate = y * 2 + (1 - zl)
    return y, zl, ring, (fwd, back, mate)


def reduce(
    turned, shared, out, sent,
    own, a_out, a_in, b_out, b_in, half_out, half_in,
    a_s, a_r, b_s, b_r, h_s, h_r,
):
    y, zl, ring, (fwd, back, mate) = group_place()
    panels = own.shape[0]

    far, near = Y // 2, Y // 2 - 1
    ahead, behind, halves = {}, {}, {}

    def product(p):
        halves_of = [
            shared[p // 2, :, :, p % 2 * 2 + k].reshape(-1, LANE) for k in range(2)
        ]
        right = jnp.concatenate(halves_of, axis=1)
        whole = jnp.dot(turned[...], right, preferred_element_type=jnp.float32)
        own[p] = whole.reshape(own.shape[1:])

    def hop(p, t):
        term = own[p, ring(far - t)]
        if t > 0:
            ahead[p].wait_recv()
            term = term + a_in[p, t - 1].astype(jnp.float32)
        a_out[p, t] = term.astype(jnp.bfloat16)
        ahead[p] = remote(a_out.at[p, t], a_in.at[p, t], a_s.at[p, t], a_r.at[p, t], "grp", fwd)
        sent.append(ahead[p])
        if t < near:
            term = own[p, ring(t - near)]
            if t > 0:
                behind[p].wait_recv()
                term = term + b_in[p, t - 1].astype(jnp.float32)
            b_out[p, t] = term.astype(jnp.bfloat16)
            behind[p] = remote(b_out.at[p, t], b_in.at[p, t], b_s.at[p, t], b_r.at[p, t], "grp", back)
            sent.append(behind[p])

    def meet(p):
        behind[p].wait_recv()
        ahead[p].wait_recv()

        def total(z):
            return (
                own[p, y, z]
                + a_in[p, far - 1, z].astype(jnp.float32)
                + b_in[p, near - 1, z].astype(jnp.float32)
            )

        half_out[p] = total(1 - zl)
        halves[p] = remote(half_out.at[p], half_in.at[p], h_s.at[p], h_r.at[p], "grp", mate)
        sent.append(halves[p])
        out[p] = total(zl)

    def finish(p):
        halves[p].wait_recv()
        out[p] = out[p] + half_in[p]

    for u in range(panels + far + 1):
        if u < panels:
            product(u)
        for p in ([u] if u < panels else []) + list(range(min(u, panels))):
            t = u - p
            if 0 <= t < far:
                hop(p, t)
            elif t == far:
                meet(p)
            elif t == far + 1:
                finish(p)


def kernel(owners, slots, scen_map, border, inverses, out, full, turned, *scratch):
    _, _, _, peers = group_place()
    first = scratch[:SHARE_REFS]
    sends = share(
        owners, slots, scen_map, border, inverses, full, turned,
        [("grp", d) for d in peers], *first
    )
    reduce(turned, full, out, sends, *scratch[SHARE_REFS:])
    for copy in sends:
        copy.wait_send()


def schur(owners, slots, scen_map, border, inverses):
    scen, depth, cols = border.shape
    parts = depth // LANE
    piece = (parts, LANE, LANE)
    chunk = (parts, ZH, LANE, LANE)
    panels, width = owners.shape[0], 2 * LANE
    rows = cols // (2 * Y)
    block = (2, rows, width)
    far, near = Y // 2, Y // 2 - 1
    f32, bf = jnp.float32, jnp.bfloat16
    dma = pltpu.SemaphoreType.DMA
    hbm = pl.BlockSpec(memory_space=pltpu.HBM)
    return pl.pallas_call(
        kernel,
        out_shape=jax.ShapeDtypeStruct((panels, rows, width), f32),
        in_specs=[hbm] * 5,
        out_specs=pl.BlockSpec(memory_space=pltpu.VMEM),
        scratch_shapes=[
            pltpu.VMEM((2, X) + chunk, bf),
            pltpu.VMEM((cols, scen * depth), bf),
            pltpu.SMEM(owners.shape, jnp.int32),
            pltpu.SMEM(slots.shape, jnp.int32),
            pltpu.SMEM(scen_map.shape, jnp.int32),
            pltpu.VMEM(border.shape, bf),
            pltpu.VMEM(inverses.shape, bf),
            dma((5,)),
            pltpu.VMEM((4, 3, TILE, LANE), bf),
            pltpu.VMEM((depth, depth), bf),
            pltpu.VMEM((X,) + chunk, bf),
            pltpu.VMEM((X,) + chunk, bf),
            pltpu.VMEM((3,) + chunk, bf),
            pltpu.VMEM((2,) + chunk, bf),
            pltpu.VMEM((3,) + chunk, bf),
            pltpu.VMEM(chunk, bf),
            pltpu.VMEM((3,) + piece, bf),
            pltpu.VMEM(piece, bf),
            pltpu.VMEM(piece, bf),
            dma((4, parts)), dma((4, parts)),
            dma((3, parts)), dma((3, parts)),
            dma((3, parts)), dma((3, parts)),
            dma((3, parts)), dma((3, parts)),
            dma((3, parts)), dma((3, parts)),
            dma((4, parts)), dma((4, parts)),
            pltpu.VMEM((panels, Y) + block, f32),
            pltpu.VMEM((panels, far) + block, bf),
            pltpu.VMEM((panels, far) + block, bf),
            pltpu.VMEM((panels, near) + block, bf),
            pltpu.VMEM((panels, near) + block, bf),
            pltpu.VMEM((panels, rows, width), f32),
            pltpu.VMEM((panels, rows, width), f32),
            dma((panels, far)), dma((panels, far)),
            dma((panels, near)), dma((panels, near)),
            dma((panels,)), dma((panels,)),
        ],
        compiler_params=pltpu.CompilerParams(
            collective_id=0, has_side_effects=True, vmem_limit_bytes=64000 * 1024
        ),
    )(owners, slots, scen_map, border, inverses)


def on_device(border, inverses, scen_map, owners, slots):
    return schur(owners, slots, scen_map, border, inverses)


def solution(mesh):
    return jax.shard_map(
        on_device,
        mesh=mesh,
        in_specs=(P("grp", None, "col"), P("grp", None, None), P("grp", None), P(), P()),
        out_specs=P(None, ("col", "grp"), None),
        check_vma=False,
    )
```

```python
import jax
import jax.numpy as jnp
from jax import lax
from jax.experimental import pallas as pl
from jax.experimental.pallas import tpu as pltpu
from jax.sharding import PartitionSpec as P

X = 4
ZH = 4
Y = 8
LANE = 128
TILE = 16
SHARE_REFS = 29


def greet(peers):
    barrier = pltpu.get_barrier_semaphore()
    for axis, peer in peers:
        pl.semaphore_signal(
            barrier, inc=1, device_id={axis: peer}, device_id_type=pl.DeviceIdType.MESH
        )
    pl.semaphore_wait(barrier, len(peers))


def remote(src, dst, send, recv, axis, peer):
    copy = pltpu.make_async_remote_copy(
        src_ref=src,
        dst_ref=dst,
        send_sem=send,
        recv_sem=recv,
        device_id={axis: peer},
        device_id_type=pl.DeviceIdType.MESH,
    )
    copy.start()
    return copy


def share(
    owners_at, slots_at, scen_map_at, border_at, inverses_at, full, turned, neighbours,
    owners, slots, scen_map, border, inverses, loads,
    marks, picked, pair_out, pair_in, x_out, x_own, x_in, z_sum, z_in, z_out, home,
    pair_s, pair_r, xs, xr, zs, zr, zgs, zgr, xgs, xgr, bs, br,
):
    fetch = [
        pltpu.make_async_copy(src, dst, loads.at[k])
        for k, (src, dst) in enumerate((
            (owners_at, owners), (slots_at, slots), (scen_map_at, scen_map),
            (border_at, border), (inverses_at, inverses),
        ))
    ]
    for copy in fetch:
        copy.start()
    at = lax.axis_index("col")
    core = lax.rem(at, 2)
    zh = lax.rem(lax.div(at, 2), ZH)
    x = lax.div(at, 2 * ZH)
    way = 1 - 2 * core
    other = 1 - core

    def col(xx, zz, cc):
        return (xx * ZH + zz) * 2 + cc

    def flag(left, right):
        same = jnp.full((TILE, LANE), left, jnp.int32) == jnp.full((TILE, LANE), right, jnp.int32)
        return jnp.where(same, 1.0, 0.0)

    scen, depth, _ = border.shape
    parts = depth // LANE
    tiles = LANE // TILE
    def panel(cc, s, r, q):
        total = None
        for k in range(3):
            start = k * 2 * LANE + (q % 2) * LANE
            block = border[s, r * LANE:(r + 1) * LANE, start:start + LANE]
            block = block.reshape(tiles, TILE, LANE)
            term = block * marks[2 * cc + q // 2, k][None]
            total = term if total is None else total + term
        return total.reshape(LANE, LANE)

    def turn(s):
        turned[:, s * depth:(s + 1) * depth] = border[s].T

    xa, xb, xf = lax.rem(x + way + X, X), lax.rem(x - way + X, X), lax.rem(x + 2, X)
    za, zb, zf = lax.rem(zh + way + ZH, ZH), lax.rem(zh - way + ZH, ZH), lax.rem(zh + 2, ZH)
    partner = col(x, zh, other)
    x_fwd, x_back = col(xa, zh, core), col(xb, zh, core)
    z_fwd, z_back = col(x, za, core), col(x, zb, core)
    for copy in fetch[:3]:
        copy.wait()
    for p in range(owners.shape[0]):
        for k in range(3):
            marks[p, k] = (flag(owners[p], at) * flag(slots[p], k)).astype(jnp.bfloat16)

    greet([("col", d) for d in (partner, x_fwd, x_back, z_fwd, z_back)] + neighbours)
    fetch[3].wait()

    order = range(parts)
    sends = []

    def send(*args):
        copy = remote(*args)
        sends.append(copy)
        return copy

    pair = {}
    for k, s in enumerate((xf, xa, xb, x)):
        for r in order:
            for q in range(ZH):
                pair_out[k, r, q] = panel(other, s, r, q)
            pair[k, r] = send(
                pair_out.at[k, r], pair_in.at[s, r], pair_s.at[k, r], pair_r.at[k, r], "col", partner
            )

    def joined(k, s, r, q):
        return panel(core, s, r, q) + pair_in[s, r, q]

    c = {}
    for k, s, peer in ((0, xf, x_fwd), (1, xb, x_back)):
        for r in order:
            pair[k, r].wait_recv()
            for q in range(ZH):
                x_out[k, r, q] = joined(k, s, r, q)
            c[k, r] = send(x_out.at[k, r], x_in.at[k, r], xs.at[k, r], xr.at[k, r], "col", peer)
    for r in order:
        pair[2, r].wait_recv()
        for q in range(ZH):
            x_own[0, r, q] = joined(2, xa, r, q)
    turn(0)
    for r in order:
        c[0, r].wait_recv()
        for q in range(ZH):
            x_out[2, r, q] = x_own[0, r, q] + x_in[0, r, q]
        c[2, r] = send(x_out.at[2, r], x_in.at[2, r], xs.at[2, r], xr.at[2, r], "col", x_fwd)
    fetch[4].wait()
    for lane in range(0, depth, LANE):
        for r in order:
            total = None
            for k in range(scen):
                mark = flag(scen_map[0, x], k).astype(jnp.bfloat16)
                block = inverses[k, r * LANE:(r + 1) * LANE, lane:lane + LANE]
                term = block.reshape(tiles, TILE, LANE) * mark[None]
                total = term if total is None else total + term
            picked[r * LANE:(r + 1) * LANE, lane:lane + LANE] = total.reshape(LANE, LANE)
    for r in order:
        pair[3, r].wait_recv()
        c[1, r].wait_recv()
        for q in range(ZH):
            x_own[1, r, q] = joined(3, x, r, q) + x_in[1, r, q]
    turn(1)

    d = {}

    def relay(r):
        d[0, r].wait_recv()
        z_out[r] = z_sum[r, za] + z_in[0, r]
        d[2, r] = send(z_out.at[r], z_in.at[2, r], zs.at[2, r], zr.at[2, r], "col", z_fwd)

    for r in order:
        c[2, r].wait_recv()
        for q in range(ZH):
            z_sum[r, q] = x_own[1, r, q] + x_in[2, r, q]
        d[0, r] = send(z_sum.at[r, zf], z_in.at[0, r], zs.at[0, r], zr.at[0, r], "col", z_fwd)
        d[1, r] = send(z_sum.at[r, zb], z_in.at[1, r], zs.at[1, r], zr.at[1, r], "col", z_back)
        if r > 0:
            relay(r - 1)
    relay(parts - 1)
    result = None
    for r in order:
        d[1, r].wait_recv()
        part = z_sum[r, zh] + z_in[1, r]
        d[2, r].wait_recv()
        part = part + z_in[2, r]
        term = jnp.dot(
            picked[:, r * LANE:(r + 1) * LANE], part, preferred_element_type=jnp.float32
        )
        result = term if result is None else result + term

    e = {}
    for r in order:
        home[r] = result[r * LANE:(r + 1) * LANE].astype(jnp.bfloat16)
        for k, peer in ((0, z_fwd), (1, z_back)):
            e[k, r] = send(
                home.at[r], full.at[core, x, r, zh], zgs.at[k, r], zgr.at[k, r], "col", peer
            )
        full[core, x, r, zh] = home[r]

    g, h = {}, {}

    def pass_on(kept, k, s, i, r, sent, got, peer):
        held = full.at[core, s, r, 2 * i:2 * i + 2]
        kept[k, i, r] = send(held, held, sent.at[k, i, r], got.at[k, i, r], "col", peer)

    def to_partner(k, s, i, r):
        pass_on(h, k, s, i, r, bs, br, partner)

    def spread_own(i, r):
        pass_on(g, 0, x, i, r, xgs, xgr, x_fwd)
        pass_on(g, 1, x, i, r, xgs, xgr, x_back)
        to_partner(0, x, i, r)

    def take_back(i):
        for r in order:
            g[0, i, r].wait_recv()
            pass_on(g, 2, xb, i, r, xgs, xgr, x_fwd)
            to_partner(1, xb, i, r)

    def take_fwd(i):
        for r in order:
            g[1, i, r].wait_recv()
            to_partner(2, xa, i, r)

    def take_far(i):
        for r in order:
            g[2, i, r].wait_recv()
            to_partner(3, xf, i, r)
        for k in range(X):
            for r in order:
                h[k, i, r].wait_recv()

    for r in order:
        e[0, r].wait_recv()
        held = full.at[core, x, r, zb]
        e[2, r] = send(held, held, zgs.at[2, r], zgr.at[2, r], "col", z_fwd)
    for r in order:
        e[1, r].wait_recv()
        e[2, r].wait_recv()
        spread_own(0, r)
    take_back(0)
    for r in order:
        spread_own(1, r)
    turn(2)
    turn(3)
    take_fwd(0)
    take_far(0)
    return sends, {1: take_back, 2: take_fwd, 3: take_far}


def group_place():
    at = lax.axis_index("grp")
    zl = lax.rem(at, 2)
    y = lax.div(at, 2)
    core = lax.rem(lax.axis_index("col"), 2)
    way = 1 - 2 * core

    def ring(step):
        return lax.rem(y + step * way + 2 * Y, Y)

    fwd, back = ring(1) * 2 + zl, ring(-1) * 2 + zl
    mate = y * 2 + (1 - zl)
    return y, zl, ring, (fwd, back, mate)


def reduce(
    turned, shared, out, sent, before,
    own, a_out, a_in, b_out, b_in, half_out, half_in,
    a_s, a_r, b_s, b_r, h_s, h_r,
):
    y, zl, ring, (fwd, back, mate) = group_place()
    panels = own.shape[0]

    far, near = Y // 2, Y // 2 - 1
    ahead, behind, halves = {}, {}, {}

    def product(p):
        halves_of = [
            shared[p // 2, :, :, p % 2 * 2 + k].reshape(-1, LANE) for k in range(2)
        ]
        right = jnp.concatenate(halves_of, axis=1)
        whole = jnp.dot(turned[...], right, preferred_element_type=jnp.float32)
        own[p] = whole.reshape(own.shape[1:])

    def hop(p, t):
        term = own[p, ring(far - t)]
        if t > 0:
            ahead[p].wait_recv()
            term = term + a_in[p, t - 1].astype(jnp.float32)
        a_out[p, t] = term.astype(jnp.bfloat16)
        ahead[p] = remote(a_out.at[p, t], a_in.at[p, t], a_s.at[p, t], a_r.at[p, t], "grp", fwd)
        sent.append(ahead[p])
        if t < near:
            term = own[p, ring(t - near)]
            if t > 0:
                behind[p].wait_recv()
                term = term + b_in[p, t - 1].astype(jnp.float32)
            b_out[p, t] = term.astype(jnp.bfloat16)
            behind[p] = remote(b_out.at[p, t], b_in.at[p, t], b_s.at[p, t], b_r.at[p, t], "grp", back)
            sent.append(behind[p])

    def meet(p):
        behind[p].wait_recv()
        ahead[p].wait_recv()

        def total(z):
            return (
                own[p, y, z]
                + a_in[p, far - 1, z].astype(jnp.float32)
                + b_in[p, near - 1, z].astype(jnp.float32)
            )

        half_out[p] = total(1 - zl)
        halves[p] = remote(half_out.at[p], half_in.at[p], h_s.at[p], h_r.at[p], "grp", mate)
        sent.append(halves[p])
        out[p] = total(zl)

    def finish(p):
        halves[p].wait_recv()
        out[p] = out[p] + half_in[p]

    starts = {0: 0, 2: 1, 1: 3, 3: 4}
    for u in range(max(starts.values()) + far + 2):
        if u in before:
            before[u](1)
        for p in reversed((0, 2, 1, 3)):
            t = u - starts[p]
            if t == 0:
                product(p)
            if 0 <= t < far:
                hop(p, t)
            elif t == far:
                meet(p)
            elif t == far + 1:
                finish(p)


def kernel(owners, slots, scen_map, border, inverses, out, full, turned, *scratch):
    _, _, _, peers = group_place()
    first = scratch[:SHARE_REFS]
    sends, later = share(
        owners, slots, scen_map, border, inverses, full, turned,
        [("grp", d) for d in peers], *first
    )
    reduce(turned, full, out, sends, later, *scratch[SHARE_REFS:])
    for copy in sends:
        copy.wait_send()


def schur(owners, slots, scen_map, border, inverses):
    scen, depth, cols = border.shape
    parts = depth // LANE
    piece = (parts, LANE, LANE)
    chunk = (parts, ZH, LANE, LANE)
    panels, width = owners.shape[0], 2 * LANE
    rows = cols // (2 * Y)
    block = (2, rows, width)
    far, near = Y // 2, Y // 2 - 1
    f32, bf = jnp.float32, jnp.bfloat16
    dma = pltpu.SemaphoreType.DMA
    hbm = pl.BlockSpec(memory_space=pltpu.HBM)
    return pl.pallas_call(
        kernel,
        out_shape=jax.ShapeDtypeStruct((panels, rows, width), f32),
        in_specs=[hbm] * 5,
        out_specs=pl.BlockSpec(memory_space=pltpu.VMEM),
        scratch_shapes=[
            pltpu.VMEM((2, X) + chunk, bf),
            pltpu.VMEM((cols, scen * depth), bf),
            pltpu.SMEM(owners.shape, jnp.int32),
            pltpu.SMEM(slots.shape, jnp.int32),
            pltpu.SMEM(scen_map.shape, jnp.int32),
            pltpu.VMEM(border.shape, bf),
            pltpu.VMEM(inverses.shape, bf),
            dma((5,)),
            pltpu.VMEM((4, 3, TILE, LANE), bf),
            pltpu.VMEM((depth, depth), bf),
            pltpu.VMEM((X,) + chunk, bf),
            pltpu.VMEM((X,) + chunk, bf),
            pltpu.VMEM((3,) + chunk, bf),
            pltpu.VMEM((2,) + chunk, bf),
            pltpu.VMEM((3,) + chunk, bf),
            pltpu.VMEM(chunk, bf),
            pltpu.VMEM((3,) + piece, bf),
            pltpu.VMEM(piece, bf),
            pltpu.VMEM(piece, bf),
            dma((4, parts)), dma((4, parts)),
            dma((3, parts)), dma((3, parts)),
            dma((3, parts)), dma((3, parts)),
            dma((3, parts)), dma((3, parts)),
            dma((3, 2, parts)), dma((3, 2, parts)),
            dma((4, 2, parts)), dma((4, 2, parts)),
            pltpu.VMEM((panels, Y) + block, f32),
            pltpu.VMEM((panels, far) + block, bf),
            pltpu.VMEM((panels, far) + block, bf),
            pltpu.VMEM((panels, near) + block, bf),
            pltpu.VMEM((panels, near) + block, bf),
            pltpu.VMEM((panels, rows, width), f32),
            pltpu.VMEM((panels, rows, width), f32),
            dma((panels, far)), dma((panels, far)),
            dma((panels, near)), dma((panels, near)),
            dma((panels,)), dma((panels,)),
        ],
        compiler_params=pltpu.CompilerParams(
            collective_id=0, has_side_effects=True, vmem_limit_bytes=64000 * 1024
        ),
    )(owners, slots, scen_map, border, inverses)


def on_device(border, inverses, scen_map, owners, slots):
    return schur(owners, slots, scen_map, border, inverses)


def solution(mesh):
    return jax.shard_map(
        on_device,
        mesh=mesh,
        in_specs=(P("grp", None, "col"), P("grp", None, None), P("grp", None), P(), P()),
        out_specs=P(None, ("col", "grp"), None),
        check_vma=False,
    )
```
